32 devices in a mesh: seq: 8 (over z, x), head: 4 (over y, core).
Axes of the slice: x: 2, y: 2, z: 4, core: 2. Of those that a mesh axis runs over, the one named last changes fastest.
Arguments:
- layer_input: bfloat16 [8192, 2048], P('seq', 'head'), may hold values from -6 to 6
- w_proj: bfloat16 [2048, 10240], P(None, 'head'), may hold values from -0.125 to 0.125
- w_beta: bfloat16 [2048, 32], P(None, 'head'), may hold values from -0.25 to 0.25
- beta_bias: float32 [32], P('head'), may hold values from -9 to 1
- d_out: bfloat16 [8192, 2048], P('seq', 'head'), may hold values from -6 to 6
Outputs:
- grad_input: bfloat16 [8192, 2048], P('seq', 'head')
- grad_proj: float32 [2048, 10240], P('seq', 'head')
- grad_beta: float32 [2048, 32], P('seq', 'head')
The draws below stay inside these ranges and needn't reach their ends.
All inputs are finite; a program needn't handle non-finite values.
Results may differ from the reference program's by a relative error of at most 0.02.
Values may be sent and summed in bfloat16 or wider, within the bound.
No kernel may reach another device: no remote copies, remote signals or barrier semaphores. Data moves between devices by JAX's collectives and lax.ppermute only.
A program may use at most 192 MiB of HBM per device.

```python
import jax
import jax.numpy as jnp
from jax import lax

D = 2048
HEADS = 16
DK = 128
SPAN = 64
TOKENS = 8192
N_HEAD = 4


def steps_of(key, extent, shards, least, largest):
    gain = 1.0
    for dim, shards_of in shards:
        draws = jax.random.uniform(jax.random.fold_in(jax.random.fold_in(key, 6), dim), (shards_of,), jnp.float32, least / len(shards), largest / len(shards))
        gain = gain * jnp.repeat(jnp.exp(draws), extent[dim] // shards_of).reshape((-1,) + (1,) * (len(extent) - 1 - dim))
    return gain


def bell_draw(stream_key, dims, deviation, bound, pieces=(), held_as=jnp.bfloat16):
    level = steps_of(stream_key, dims, pieces, -0.22, 0.18) if pieces else 1.0
    array = jax.random.normal(stream_key, dims, jnp.float32) * deviation * level
    return jnp.minimum(jnp.maximum(array, -bound), bound).astype(held_as)


def setup_inputs(seed: int = 0) -> dict:
    splits = jax.random.split(jax.random.key(seed), 6)
    layer_input = bell_draw(splits[0], (TOKENS, D), 1.0, 6.0, ((0, 8), (1, 4)))
    w_proj = bell_draw(splits[1], (D, HEADS * 5 * DK), D ** -0.5, 0.125, ((1, 4),))
    w_beta = bell_draw(splits[2], (D, HEADS * 2), (D // 4) ** -0.5, 0.25, ((1, 4),))
    beta_bias = jnp.clip(-9.0 + 10.0 * jax.random.uniform(splits[3], (HEADS * 2,), jnp.float32) ** steps_of(splits[3], (HEADS * 2,), ((0, 4),), -0.2, 0.2), -9.0, 1.0)
    d_out = bell_draw(splits[4], (TOKENS, HEADS * DK), 1.0, 6.0, ((0, 8), (1, 4)))
    return dict(layer_input=layer_input, w_proj=w_proj, w_beta=w_beta, beta_bias=beta_bias, d_out=d_out)


MAX_PRECISION = lax.Precision.HIGHEST

def prepare(projected, logits):
    length = projected.shape[0]
    head_count = logits.shape[1] // 2
    blocks = length // SPAN
    sections = projected.reshape(length, head_count, 5, DK)
    queries = jnp.transpose(sections[:, :, 0], (1, 0, 2)).reshape(head_count, blocks, SPAN, DK)
    raw_keys = jnp.transpose(sections[:, :, 1:3], (1, 0, 2, 3)).reshape(head_count, blocks, 2 * SPAN, DK)
    values = jnp.transpose(sections[:, :, 3:5], (1, 0, 2, 3)).reshape(head_count, blocks, 2 * SPAN, DK)
    scaled_keys = raw_keys * lax.rsqrt(lax.optimization_barrier(jnp.sum(raw_keys * raw_keys, axis=-1, keepdims=True)) + 1e-06)
    strengths = 2.0 * jax.nn.sigmoid(jnp.transpose(logits.reshape(length, head_count, 2), (1, 0, 2)).reshape(head_count, blocks, 2 * SPAN))
    intersections = jnp.einsum('hcik,hcjk->hcij', scaled_keys, scaled_keys, precision=MAX_PRECISION)
    lower_part = jnp.tril(strengths[..., :, None] * intersections, -1)
    system = lower_part + jnp.eye(2 * SPAN, dtype=jnp.float32)
    targets = strengths[..., None] * jnp.concatenate([scaled_keys, values], axis=-1)
    solved = jax.scipy.linalg.solve_triangular(system, targets, lower=True)
    return (queries, scaled_keys, solved[..., :DK], solved[..., DK:])

def run_spans(queries, scaled_keys, weights_w, updates, initial):
    read_index = jnp.arange(SPAN, dtype=jnp.int32)[:, None]
    writes = jnp.arange(2 * SPAN, dtype=jnp.int32)[None, :]
    visible = (writes <= 2 * read_index + 1).astype(jnp.float32)

    def advance(carried_state, inputs):
        query_tile, key_tile, wide_tile, update_tile = inputs
        delta_rows = update_tile - jnp.einsum('lyx,lxg->lyg', wide_tile, carried_state, precision=MAX_PRECISION)
        score_matrix = jnp.einsum('hik,hjk->hij', query_tile, key_tile, precision=MAX_PRECISION) * visible
        produced_output = jnp.einsum('lyx,lxg->lyg', query_tile, carried_state, precision=MAX_PRECISION) + jnp.einsum('sml,slo->smo', score_matrix, delta_rows, precision=MAX_PRECISION)
        carried_state = carried_state + jnp.einsum('qnz,qna->qza', key_tile, delta_rows, precision=MAX_PRECISION)
        return (carried_state, produced_output)
    stacked = tuple((jnp.moveaxis(member, 1, 0) for member in (queries, scaled_keys, weights_w, updates)))
    final_state, produced_output = lax.scan(advance, initial, stacked)
    head_count = initial.shape[0]
    outputs = jnp.transpose(produced_output, (0, 2, 1, 3)).reshape(-1, head_count * DK)
    return (outputs, final_state)

def group_terms(layer_input, w_proj, w_beta, beta_bias, d_out, group_index):
    head_count = HEADS // N_HEAD
    columns = head_count * 5 * DK
    w_group = lax.dynamic_slice_in_dim(w_proj, group_index * columns, columns, 1)
    rate_group = lax.dynamic_slice_in_dim(w_beta, group_index * 2 * head_count, 2 * head_count, 1)
    bias_group = lax.dynamic_slice_in_dim(beta_bias, group_index * 2 * head_count, 2 * head_count, 0)
    cotangent = lax.dynamic_slice_in_dim(d_out, group_index * head_count * DK, head_count * DK, 1)
    projected = jnp.dot(layer_input.astype(jnp.float32), w_group.astype(jnp.float32), preferred_element_type=jnp.float32).astype(jnp.bfloat16)
    logits = jnp.dot(layer_input.astype(jnp.float32), rate_group.astype(jnp.float32), preferred_element_type=jnp.float32) + bias_group
    stored = lax.optimization_barrier(projected)
    prepared, pull_prepare = jax.vjp(prepare, stored.astype(jnp.float32), logits)
    initial = jnp.zeros((head_count, DK, DK), jnp.float32)
    (outputs, final_state), pull_run = jax.vjp(run_spans, prepared[0], prepared[1], prepared[2], prepared[3], initial)
    pulled = pull_run((cotangent.astype(jnp.float32), jnp.zeros_like(final_state)))
    grad_projected, grad_logits = pull_prepare(pulled[:4])
    grad_projected = grad_projected.astype(jnp.bfloat16)
    grad_logits = grad_logits.astype(jnp.bfloat16)
    partial_input = jnp.dot(grad_projected.astype(jnp.float32), w_group.T.astype(jnp.float32), preferred_element_type=jnp.float32) + jnp.dot(grad_logits.astype(jnp.float32), rate_group.T.astype(jnp.float32), preferred_element_type=jnp.float32)
    grad_weights = jnp.dot(layer_input.T.astype(jnp.float32), grad_projected.astype(jnp.float32), preferred_element_type=jnp.float32)
    grad_rates = jnp.dot(layer_input.T.astype(jnp.float32), grad_logits.astype(jnp.float32), preferred_element_type=jnp.float32)
    return (partial_input, grad_weights, grad_rates)

def reference(layer_input, w_proj, w_beta, beta_bias, d_out):

    def visit(summed, group_index):
        partial_input, grad_weights, grad_rates = group_terms(layer_input, w_proj, w_beta, beta_bias, d_out, group_index)
        rounded = lax.optimization_barrier(partial_input.astype(jnp.bfloat16))
        return (summed + rounded.astype(jnp.float32), (grad_weights, grad_rates))
    summed, (weight_stack, rate_stack) = lax.scan(visit, jnp.zeros(layer_input.shape, jnp.float32), jnp.arange(N_HEAD, dtype=jnp.int32))
    grad_proj = jnp.transpose(weight_stack, (1, 0, 2)).reshape(D, -1)
    grad_beta = jnp.transpose(rate_stack, (1, 0, 2)).reshape(D, -1)
    return (summed.astype(jnp.bfloat16), grad_proj, grad_beta)
```

```python
import functools

import jax
import jax.numpy as jnp
import numpy as np
from jax import lax
from jax.experimental import pallas as pl
from jax.experimental.pallas import tpu as pltpu
from jax.sharding import PartitionSpec as P

DK = 128
SPAN = 64
ROWS = 2 * SPAN
BASE = 16
HALF = BASE // 2
COLS = 5 * DK
BF = jnp.bfloat16
F32 = jnp.float32
VMEM_LIMIT = 56 << 20


def dot(a, b, ca, cb):
    return lax.dot_general(
        a.astype(BF), b.astype(BF), (((ca,), (cb,)), ((), ())), preferred_element_type=F32
    )


def nn(a, b):
    return dot(a, b, 1, 0)


def nt(a, b):
    return dot(a, b, 1, 1)


def tn(a, b):
    return dot(a, b, 0, 0)


def split(a):
    high = a.astype(BF)
    return high, (a - high.astype(F32)).astype(BF)


def nn3(a, b):
    ah, al = split(a)
    bh, bl = split(b)
    return nn(jnp.concatenate([ah, al], 1), jnp.concatenate([bh, bh], 0)) + nn(ah, bl)


def nt3(a, b):
    ah, al = split(a)
    bh, bl = split(b)
    return nt(jnp.concatenate([ah, al], 1), jnp.concatenate([bh, bh], 1)) + nt(ah, bl)


def rows_cols(rows, cols):
    row = lax.broadcasted_iota(jnp.int32, (rows, cols), 0)
    col = lax.broadcasted_iota(jnp.int32, (rows, cols), 1)
    return row, col


def order(index):
    return 2 * (index % SPAN) + index // SPAN


def strict_mask():
    row, col = rows_cols(ROWS, ROWS)
    return order(col) < order(row)


def visible_mask():
    row, col = rows_cols(SPAN, ROWS)
    return col % SPAN <= row


def stack_steps(ref, rows, first):
    return jnp.concatenate(
        [ref[rows, first * DK : (first + 1) * DK], ref[rows, (first + 1) * DK : (first + 2) * DK]], 0
    ).astype(F32)


def strengths_of(logit_ref, rows):
    pair = logit_ref[0, rows, :]
    return 2.0 * jax.nn.sigmoid(jnp.concatenate([pair[:, 0:1], pair[:, 1:2]], 0))


def spread_table():
    table = np.zeros((DK, BASE, DK), np.float32)
    for lane in range(DK):
        group = (lane % SPAN) // HALF
        for member in range(BASE):
            source = (member // HALF) * SPAN + group * HALF + member % HALF
            table[source, member, lane] = 1.0
    return table.reshape(DK, BASE * DK)


def local_kernel(
    blocks,
    unroll,
    spread_ref,
    proj_ref,
    logit_ref,
    grad_ref,
    key_ref,
    inv_ref,
    wide_ref,
    upd_ref,
    read_ref,
    map_ref,
    shift_ref,
    source_ref,
    total_ref,
    system,
    packed,
    coef,
    solved,
    maps,
    shifts,
    sources,
):
    strict = strict_mask()
    lane_group = (rows_cols(HALF, ROWS)[1] % SPAN) // HALF

    def first(outer, carry):
        for inner in range(unroll):
            block = outer * unroll + inner
            rows = pl.ds(pl.multiple_of(block * SPAN, SPAN), SPAN)
            raw = stack_steps(proj_ref, rows, 1)
            strengths = strengths_of(logit_ref, rows)
            keys = raw * lax.rsqrt(jnp.sum(raw * raw, axis=1, keepdims=True) + 1e-06)
            key_ref[0, block] = keys.astype(BF)
            lower = jnp.where(strict, strengths * nt3(keys, keys), 0.0)
            system[block] = lower
            for step in range(2):
                piece = jnp.zeros((HALF, ROWS), F32)
                for group in range(SPAN // HALF):
                    start = step * SPAN + group * HALF
                    piece = jnp.where(lane_group == group, lower[start : start + HALF], piece)
                packed[pl.ds(step * HALF * blocks + block, HALF, stride=blocks), :] = piece
        return carry

    lax.fori_loop(0, blocks // unroll, first, 0)

    high, low = split(packed[...])
    spread = spread_ref[...]
    coef[...] = nn(jnp.concatenate([high, low], 1), jnp.concatenate([spread, spread], 0))
    lane = rows_cols(blocks, ROWS)[1]
    found = {}
    for when in range(BASE):
        step, tick = when % 2, when // 2
        here = step * HALF + tick
        value = jnp.where((lane // SPAN == step) & (lane % HALF == tick), 1.0, 0.0)
        for before in range(when):
            there = (before % 2) * HALF + before // 2
            weight = coef[here * blocks : (here + 1) * blocks, there * ROWS : (there + 1) * ROWS]
            value = value - weight * found[before]
        found[when] = value
        solved[here * blocks : (here + 1) * blocks, :] = value

    row, col = rows_cols(ROWS, ROWS)
    row_time, col_time = order(row), order(col)
    visible = visible_mask()

    def second(outer, carry):
        for inner in range(unroll):
            block = outer * unroll + inner
            rows = pl.ds(pl.multiple_of(block * SPAN, SPAN), SPAN)
            pieces = []
            for step in range(2):
                piece = solved[pl.ds(step * HALF * blocks + block, HALF, stride=blocks), :]
                for group in range(SPAN // HALF):
                    pieces.append(jnp.where(lane_group == group, piece, 0.0))
            inverse = jnp.concatenate(pieces, 0)
            lower = system[block]
            size = BASE
            while size < ROWS:
                joins = (row_time // (2 * size) == col_time // (2 * size)) & (
                    row_time // size != col_time // size
                )
                inverse = inverse - nn3(inverse, nn3(jnp.where(joins, lower, 0.0), inverse))
                size *= 2
            strengths = strengths_of(logit_ref, rows)
            keys = key_ref[0, block]
            values = stack_steps(proj_ref, rows, 3)
            query = proj_ref[rows, 0:DK]
            cotangent = grad_ref[rows, :]
            inverse_bf = inverse.astype(BF)
            inv_ref[0, block] = inverse_bf
            targets = jnp.concatenate([strengths * keys.astype(F32), strengths * values], 1)
            both = nn(inverse_bf, targets)
            both_bf = both.astype(BF)
            wide_bf = both_bf[:, :DK]
            wide_ref[0, block] = wide_bf
            upd_ref[0, block] = both_bf[:, DK:]
            score = jnp.where(visible, nt(query, keys), 0.0)
            reads = tn(score, cotangent)
            read_ref[0, block] = reads.astype(BF)
            folded = tn(keys, both_bf)
            maps[block] = -folded[:, :DK]
            shifts[block] = folded[:, DK:]
            sources[block] = tn(query, cotangent) - tn(wide_bf, reads)
        return carry

    lax.fori_loop(0, blocks // unroll, second, 0)

    offset, count = 0, blocks
    while count > 1:
        for pair in range(count // 2):
            left, right, parent = offset + 2 * pair, offset + 2 * pair + 1, offset + count + pair
            near, far = maps[left], maps[right]
            joined = nn(far, jnp.concatenate([near, shifts[left]], 1))
            maps[parent] = near + far + joined[:, :DK]
            shifts[parent] = shifts[left] + shifts[right] + joined[:, DK:]
            later = sources[right]
            sources[parent] = sources[left] + later + tn(near, later)
        offset += count
        count //= 2
    map_ref[0] = maps[...].astype(BF)
    shift_ref[0] = shifts[...].astype(BF)
    source_ref[0] = sources[...].astype(BF)
    total_ref[0, 0] = maps[offset]
    total_ref[0, 1] = shifts[offset]
    total_ref[0, 2] = sources[offset]


def params():
    return pltpu.CompilerParams(
        dimension_semantics=("arbitrary",), vmem_limit_bytes=VMEM_LIMIT
    )


def local_pass(projected, logits, d_out, first_head, heads):
    tokens = projected.shape[0]
    blocks = tokens // SPAN
    nodes = 2 * blocks - 1
    square = jax.ShapeDtypeStruct((heads, blocks, ROWS, DK), BF)
    tree = jax.ShapeDtypeStruct((heads, nodes, DK, DK), BF)
    tile = pl.BlockSpec((1, blocks, ROWS, DK), lambda h: (h, 0, 0, 0))
    branch = pl.BlockSpec((1, nodes, DK, DK), lambda h: (h, 0, 0, 0))
    unroll = 2
    return pl.pallas_call(
        functools.partial(local_kernel, blocks, unroll),
        grid=(heads,),
        out_shape=(square,) * 5
        + (tree,) * 3
        + (jax.ShapeDtypeStruct((heads, 3, DK, DK), F32),),
        in_specs=[
            pl.BlockSpec((DK, BASE * DK), lambda h: (0, 0)),
            pl.BlockSpec((tokens, COLS), lambda h: (0, first_head + h)),
            pl.BlockSpec((1, tokens, 2), lambda h: (first_head + h, 0, 0)),
            pl.BlockSpec((tokens, DK), lambda h: (0, first_head + h)),
        ],
        out_specs=(tile,) * 5
        + (branch,) * 3
        + (pl.BlockSpec((1, 3, DK, DK), lambda h: (h, 0, 0, 0)),),
        scratch_shapes=[
            pltpu.VMEM((blocks, ROWS, ROWS), F32),
            pltpu.VMEM((BASE * blocks, ROWS), F32),
            pltpu.VMEM((BASE * blocks, BASE * ROWS), F32),
            pltpu.VMEM((BASE * blocks, ROWS), F32),
            pltpu.VMEM((nodes, DK, DK), F32),
            pltpu.VMEM((nodes, DK, DK), F32),
            pltpu.VMEM((nodes, DK, DK), F32),
        ],
        compiler_params=params(),
        cost_estimate=pl.CostEstimate(
            flops=heads * blocks * 60 * DK**3, bytes_accessed=heads * 8 << 20, transcendentals=0
        ),
        name="local_pass",
    )(jnp.asarray(spread_table(), BF), projected, logits, d_out)


def grad_kernel(
    blocks,
    unroll,
    proj_ref,
    logit_ref,
    grad_ref,
    key_ref,
    inv_ref,
    wide_ref,
    upd_ref,
    read_ref,
    map_ref,
    shift_ref,
    source_ref,
    edge_ref,
    out_ref,
    rate_ref,
    states,
    ends,
):
    nodes = 2 * blocks - 1
    states[nodes - 1] = edge_ref[0, 0]
    ends[nodes - 1] = edge_ref[0, 1]
    count, offset = 2, nodes - 3
    while count <= blocks:
        for pair in range(count // 2):
            left, right, parent = offset + 2 * pair, offset + 2 * pair + 1, offset + count + pair
            state, end = states[parent], ends[parent]
            states[left] = state
            states[right] = state + nn(map_ref[0, left], state) + shift_ref[0, left].astype(F32)
            ends[right] = end
            ends[left] = end + tn(map_ref[0, right], end) + source_ref[0, right].astype(F32)
        count *= 2
        offset -= count

    strict = strict_mask()
    visible = visible_mask()

    def body(outer, carry):
        for inner in range(unroll):
            block = outer * unroll + inner
            rows = pl.ds(pl.multiple_of(block * SPAN, SPAN), SPAN)
            raw = stack_steps(proj_ref, rows, 1)
            scale = lax.rsqrt(jnp.sum(raw * raw, axis=1, keepdims=True) + 1e-06)
            keys = raw * scale
            keys_bf = key_ref[0, block]
            strengths = strengths_of(logit_ref, rows)
            values = stack_steps(proj_ref, rows, 3)
            query = proj_ref[rows, 0:DK]
            cotangent = grad_ref[rows, :]
            state = states[block].astype(BF)
            end = ends[block].astype(BF)
            delta = (upd_ref[0, block].astype(F32) - nn(wide_ref[0, block], state)).astype(BF)
            back = read_ref[0, block].astype(F32) + nn(keys_bf, end)
            held = tn(inv_ref[0, block], back)
            many = nt(
                jnp.concatenate([cotangent, held.astype(BF)], 0),
                jnp.concatenate([delta, state], 0),
            )
            seen = jnp.where(visible, many[:SPAN, :ROWS], 0.0).astype(BF)
            crossed = jnp.where(strict, many[SPAN:, :ROWS], 0.0).astype(BF)
            onward = nn(jnp.concatenate([seen, crossed], 0), keys_bf)
            d_query = many[:SPAN, ROWS:] + onward[:SPAN]
            inner_sum = many[SPAN:, ROWS:] + onward[SPAN:]
            d_keys = (
                tn(
                    jnp.concatenate([seen, crossed], 0),
                    jnp.concatenate([query, (-strengths * keys).astype(BF)], 0),
                )
                + nt(delta, end)
                - strengths * inner_sum
            )
            d_values = strengths * held
            d_rate = jnp.sum(held * values - keys * inner_sum, axis=1, keepdims=True)
            d_raw = scale * (d_keys - keys * jnp.sum(keys * d_keys, axis=1, keepdims=True))
            d_logit = d_rate * strengths * (1.0 - 0.5 * strengths)
            out_ref[rows, 0:DK] = d_query.astype(BF)
            out_ref[rows, DK : 2 * DK] = d_raw[:SPAN].astype(BF)
            out_ref[rows, 2 * DK : 3 * DK] = d_raw[SPAN:].astype(BF)
            out_ref[rows, 3 * DK : 4 * DK] = d_values[:SPAN].astype(BF)
            out_ref[rows, 4 * DK : 5 * DK] = d_values[SPAN:].astype(BF)
            rate_ref[0, rows, :] = jnp.concatenate([d_logit[:SPAN], d_logit[SPAN:]], 1)
        return carry

    lax.fori_loop(0, blocks // unroll, body, 0)


def grad_pass(projected, logits, d_out, kept, edges, first_head, heads):
    tokens = projected.shape[0]
    blocks = tokens // SPAN
    nodes = 2 * blocks - 1
    tile = pl.BlockSpec((1, blocks, ROWS, DK), lambda h: (h, 0, 0, 0))
    branch = pl.BlockSpec((1, nodes, DK, DK), lambda h: (h, 0, 0, 0))
    unroll = 2
    return pl.pallas_call(
        functools.partial(grad_kernel, blocks, unroll),
        grid=(heads,),
        out_shape=(
            jax.ShapeDtypeStruct((tokens, heads * COLS), BF),
            jax.ShapeDtypeStruct((heads, tokens, 2), F32),
        ),
        in_specs=[
            pl.BlockSpec((tokens, COLS), lambda h: (0, first_head + h)),
            pl.BlockSpec((1, tokens, 2), lambda h: (first_head + h, 0, 0)),
            pl.BlockSpec((tokens, DK), lambda h: (0, first_head + h)),
        ]
        + [tile] * 5
        + [branch] * 3
        + [pl.BlockSpec((1, 2, DK, DK), lambda h: (h, 0, 0, 0))],
        out_specs=(
            pl.BlockSpec((tokens, COLS), lambda h: (0, h)),
            pl.BlockSpec((1, tokens, 2), lambda h: (h, 0, 0)),
        ),
        scratch_shapes=[
            pltpu.VMEM((nodes, DK, DK), F32),
            pltpu.VMEM((nodes, DK, DK), F32),
        ],
        compiler_params=params(),
        cost_estimate=pl.CostEstimate(
            flops=heads * blocks * 30 * DK**3, bytes_accessed=heads * 8 << 20, transcendentals=0
        ),
        name="grad_pass",
    )(projected, logits, d_out, *kept, edges)


def bmm(a, b):
    return jnp.einsum("hij,hjk->hik", a.astype(BF), b.astype(BF), preferred_element_type=F32)


def bmm_t(a, b):
    return jnp.einsum("hji,hjk->hik", a.astype(BF), b.astype(BF), preferred_element_type=F32)


def shifted(value, by):
    devices = lax.axis_size("seq")
    pairs = [(i, i + by) for i in range(devices) if 0 <= i + by < devices]
    return lax.ppermute(value.astype(BF), "seq", pairs).astype(F32)


def exchange(total):
    devices = lax.axis_size("seq")
    tail_map, tail_shift, head_source = total[:, 0], total[:, 1], total[:, 2]
    head_map = tail_map
    past_map = past_shift = next_map = next_source = None
    by = 1
    while by < devices:
        last = 2 * by >= devices
        if last:
            got_shift = shifted(tail_shift, by)
            got_source = shifted(head_source, -by)
        else:
            behind = shifted(jnp.concatenate([tail_map, tail_shift], 2), by)
            ahead = shifted(jnp.concatenate([head_map, head_source], 2), -by)
            got_map, got_shift = behind[:, :, :DK], behind[:, :, DK:]
            got_next, got_source = ahead[:, :, :DK], ahead[:, :, DK:]
        if past_map is None:
            past_shift, next_source = got_shift, got_source
        else:
            past_shift = past_shift + got_shift + bmm(past_map, got_shift)
            next_source = next_source + got_source + bmm_t(next_map, got_source)
        if not last:
            if past_map is None:
                past_map, next_map = got_map, got_next
            else:
                past_map = past_map + got_map + bmm(past_map, got_map)
                next_map = next_map + got_next + bmm(got_next, next_map)
            tail_shift = tail_shift + got_shift + bmm(tail_map, got_shift)
            head_source = head_source + got_source + bmm_t(head_map, got_source)
            tail_map = tail_map + got_map + bmm(tail_map, got_map)
            head_map = head_map + got_next + bmm(got_next, head_map)
        by *= 2
    return jnp.stack([past_shift, next_source], 1)


def shards(layer_input, w_proj, w_beta, beta_bias, d_out):
    whole = lax.all_gather(layer_input, "head", axis=1, tiled=True)
    tokens = whole.shape[0]
    heads = w_beta.shape[1] // 2
    projected = jnp.dot(whole, w_proj, preferred_element_type=F32).astype(BF)
    logits = jnp.dot(whole, w_beta, preferred_element_type=F32) + beta_bias
    logits = jnp.transpose(logits.reshape(tokens, heads, 2), (1, 0, 2))
    *kept, total = local_pass(projected, logits, d_out, 0, heads)
    edges = exchange(total)
    grad_projected, grad_logits = grad_pass(projected, logits, d_out, kept, edges, 0, heads)
    grad_logits = jnp.transpose(grad_logits, (1, 0, 2)).reshape(tokens, 2 * heads).astype(BF)
    partial_input = jnp.einsum(
        "tc,dc->td", grad_projected, w_proj, preferred_element_type=F32
    ) + jnp.einsum("tc,dc->td", grad_logits, w_beta, preferred_element_type=F32)
    grad_input = lax.psum_scatter(
        partial_input.astype(BF), "head", scatter_dimension=1, tiled=True
    )
    grad_weights = jnp.einsum("td,tc->dc", whole, grad_projected, preferred_element_type=F32)
    grad_rates = jnp.einsum("td,tc->dc", whole, grad_logits, preferred_element_type=F32)
    grad_proj = lax.psum_scatter(grad_weights.astype(BF), "seq", scatter_dimension=0, tiled=True)
    grad_beta = lax.psum_scatter(grad_rates.astype(BF), "seq", scatter_dimension=0, tiled=True)
    return (grad_input, grad_proj.astype(F32), grad_beta.astype(F32))


def solution(mesh):
    in_specs = (P("seq", "head"), P(None, "head"), P(None, "head"), P("head"), P("seq", "head"))
    out_specs = (P("seq", "head"), P("seq", "head"), P("seq", "head"))
    return jax.shard_map(shards, mesh=mesh, in_specs=in_specs, out_specs=out_specs, check_vma=False)
```

```python
import functools

import jax
import jax.numpy as jnp
import numpy as np
from jax import lax
from jax.experimental import pallas as pl
from jax.experimental.pallas import tpu as pltpu
from jax.sharding import PartitionSpec as P

DK = 128
SPAN = 64
ROWS = 2 * SPAN
BASE = 16
HALF = BASE // 2
COLS = 5 * DK
BF = jnp.bfloat16
F32 = jnp.float32
VMEM_LIMIT = 56 << 20


def dot(a, b, ca, cb):
    return lax.dot_general(
        a.astype(BF), b.astype(BF), (((ca,), (cb,)), ((), ())), preferred_element_type=F32
    )


def nn(a, b):
    return dot(a, b, 1, 0)


def nt(a, b):
    return dot(a, b, 1, 1)


def tn(a, b):
    return dot(a, b, 0, 0)


def split(a):
    high = a.astype(BF)
    return high, (a - high.astype(F32)).astype(BF)


def nn3(a, b):
    ah, al = split(a)
    bh, bl = split(b)
    return nn(jnp.concatenate([ah, al], 1), jnp.concatenate([bh, bh], 0)) + nn(ah, bl)


def nt3(a, b):
    ah, al = split(a)
    bh, bl = split(b)
    return nt(jnp.concatenate([ah, al], 1), jnp.concatenate([bh, bh], 1)) + nt(ah, bl)


def rows_cols(rows, cols):
    row = lax.broadcasted_iota(jnp.int32, (rows, cols), 0)
    col = lax.broadcasted_iota(jnp.int32, (rows, cols), 1)
    return row, col


def order(index):
    return 2 * (index % SPAN) + index // SPAN


def strict_mask():
    row, col = rows_cols(ROWS, ROWS)
    return order(col) < order(row)


def visible_mask():
    row, col = rows_cols(SPAN, ROWS)
    return col % SPAN <= row


def stack_steps(ref, rows, first):
    return jnp.concatenate(
        [ref[rows, first * DK : (first + 1) * DK], ref[rows, (first + 1) * DK : (first + 2) * DK]], 0
    ).astype(F32)


def strengths_of(logit_ref, rows, head):
    pair = logit_ref[rows, 2 * head : 2 * head + 2]
    return 2.0 * jax.nn.sigmoid(jnp.concatenate([pair[:, 0:1], pair[:, 1:2]], 0))


def spread_table():
    table = np.zeros((DK, BASE, DK), np.float32)
    for lane in range(DK):
        group = (lane % SPAN) // HALF
        for member in range(BASE):
            source = (member // HALF) * SPAN + group * HALF + member % HALF
            table[source, member, lane] = 1.0
    return table.reshape(DK, BASE * DK)


def local_kernel(
    blocks,
    unroll,
    marks,
    head,
    spread_ref,
    proj_ref,
    logit_ref,
    grad_ref,
    *rest,
):
    (
    key_ref,
    inv_ref,
    wide_ref,
    upd_ref,
    read_ref,
    map_ref,
    shift_ref,
    source_ref,
    total_ref,
    system,
    packed,
    coef,
    solved,
    maps,
    shifts,
    sources,
    ) = rest[marks:]
    strict = strict_mask()
    lane_group = (rows_cols(HALF, ROWS)[1] % SPAN) // HALF

    def first(outer, carry):
        for inner in range(unroll):
            block = outer * unroll + inner
            rows = pl.ds(pl.multiple_of(block * SPAN, SPAN), SPAN)
            raw = stack_steps(proj_ref, rows, 1)
            strengths = strengths_of(logit_ref, rows, head)
            keys = raw * lax.rsqrt(jnp.sum(raw * raw, axis=1, keepdims=True) + 1e-06)
            key_ref[0, block] = keys.astype(BF)
            lower = jnp.where(strict, strengths * nt3(keys, keys), 0.0)
            system[block] = lower
            for step in range(2):
                piece = jnp.zeros((HALF, ROWS), F32)
                for group in range(SPAN // HALF):
                    start = step * SPAN + group * HALF
                    piece = jnp.where(lane_group == group, lower[start : start + HALF], piece)
                packed[pl.ds(step * HALF * blocks + block, HALF, stride=blocks), :] = piece
        return carry

    lax.fori_loop(0, blocks // unroll, first, 0)

    high, low = split(packed[...])
    spread = spread_ref[...]
    coef[...] = nn(jnp.concatenate([high, low], 1), jnp.concatenate([spread, spread], 0))
    lane = rows_cols(blocks, ROWS)[1]
    found = {}
    for when in range(BASE):
        step, tick = when % 2, when // 2
        here = step * HALF + tick
        value = jnp.where((lane // SPAN == step) & (lane % HALF == tick), 1.0, 0.0)
        for before in range(when):
            there = (before % 2) * HALF + before // 2
            weight = coef[here * blocks : (here + 1) * blocks, there * ROWS : (there + 1) * ROWS]
            value = value - weight * found[before]
        found[when] = value
        solved[here * blocks : (here + 1) * blocks, :] = value

    row, col = rows_cols(ROWS, ROWS)
    row_time, col_time = order(row), order(col)
    visible = visible_mask()

    joins = []
    size = BASE
    while size < ROWS:
        joins.append(
            (row_time // (2 * size) == col_time // (2 * size))
            & (row_time // size != col_time // size)
        )
        size *= 2

    def second(outer, carry):
        own = [outer * unroll + inner for inner in range(unroll)]
        rows = [pl.ds(pl.multiple_of(block * SPAN, SPAN), SPAN) for block in own]
        inverse = []
        for block in own:
            pieces = []
            for step in range(2):
                piece = solved[pl.ds(step * HALF * blocks + block, HALF, stride=blocks), :]
                for group in range(SPAN // HALF):
                    pieces.append(jnp.where(lane_group == group, piece, 0.0))
            inverse.append(jnp.concatenate(pieces, 0))
        for join in joins:
            half = [
                nn3(jnp.where(join, system[block], 0.0), inv) for block, inv in zip(own, inverse)
            ]
            inverse = [inv - nn3(inv, x) for inv, x in zip(inverse, half)]
        inverse = [inv.astype(BF) for inv in inverse]
        scores = [
            jnp.where(visible, nt(proj_ref[r, 0:DK], key_ref[0, block]), 0.0).astype(BF)
            for block, r in zip(own, rows)
        ]
        reads = [tn(score, grad_ref[r, :]).astype(BF) for score, r in zip(scores, rows)]
        both = []
        for block, r, inv in zip(own, rows, inverse):
            inv_ref[0, block] = inv
            strengths = strengths_of(logit_ref, r, head)
            keys = key_ref[0, block].astype(F32)
            values = stack_steps(proj_ref, r, 3)
            targets = jnp.concatenate([strengths * keys, strengths * values], 1)
            both.append(nn(inv, targets).astype(BF))
        folded = [tn(key_ref[0, block], x) for block, x in zip(own, both)]
        gained = [
            tn(proj_ref[r, 0:DK], grad_ref[r, :]) - tn(x[:, :DK], read)
            for r, x, read in zip(rows, both, reads)
        ]
        for block, x, read, fold, gain in zip(own, both, reads, folded, gained):
            wide_ref[0, block] = x[:, :DK]
            upd_ref[0, block] = x[:, DK:]
            read_ref[0, block] = read
            maps[block] = -fold[:, :DK]
            shifts[block] = fold[:, DK:]
            sources[block] = gain
        return carry

    lax.fori_loop(0, blocks // unroll, second, 0)

    offset, count = 0, blocks
    while count > 1:
        half = count // 2
        lefts = [offset + 2 * pair for pair in range(half)]
        joined = [
            nn(maps[left + 1], jnp.concatenate([maps[left], shifts[left]], 1)) for left in lefts
        ]
        moved = [tn(maps[left], sources[left + 1]) for left in lefts]
        for pair, left in enumerate(lefts):
            parent = offset + count + pair
            maps[parent] = maps[left] + maps[left + 1] + joined[pair][:, :DK]
            shifts[parent] = shifts[left] + shifts[left + 1] + joined[pair][:, DK:]
            sources[parent] = sources[left] + sources[left + 1] + moved[pair]
        offset += count
        count //= 2
    map_ref[0] = maps[...].astype(BF)
    shift_ref[0] = shifts[...].astype(BF)
    source_ref[0] = sources[...].astype(BF)
    total_ref[0, 0] = maps[offset]
    total_ref[0, 1] = shifts[offset]
    total_ref[0, 2] = sources[offset]


def divisor(blocks, most):
    while blocks % most:
        most //= 2
    return most


def params():
    return pltpu.CompilerParams(
        dimension_semantics=("arbitrary",), vmem_limit_bytes=VMEM_LIMIT
    )


def local_pass(projected, logits, d_out, head, marks=()):
    tokens = projected.shape[0]
    blocks = tokens // SPAN
    nodes = 2 * blocks - 1
    square = jax.ShapeDtypeStruct((1, blocks, ROWS, DK), BF)
    tree = jax.ShapeDtypeStruct((1, nodes, DK, DK), BF)
    tile = pl.BlockSpec((1, blocks, ROWS, DK), lambda h: (h, 0, 0, 0))
    branch = pl.BlockSpec((1, nodes, DK, DK), lambda h: (h, 0, 0, 0))
    unroll = divisor(blocks, 16)
    return pl.pallas_call(
        functools.partial(local_kernel, blocks, unroll, len(marks), head),
        grid=(1,),
        out_shape=(square,) * 5
        + (tree,) * 3
        + (jax.ShapeDtypeStruct((1, 3, DK, DK), F32),),
        in_specs=[
            pl.BlockSpec((DK, BASE * DK), lambda h: (0, 0)),
            pl.BlockSpec((tokens, COLS), lambda h: (0, h)),
            pl.BlockSpec((tokens, logits.shape[1]), lambda h: (0, 0)),
            pl.BlockSpec((tokens, DK), lambda h: (0, head)),
        ]
        + [pl.BlockSpec(memory_space=pl.ANY)] * len(marks),
        out_specs=(tile,) * 5
        + (branch,) * 3
        + (pl.BlockSpec((1, 3, DK, DK), lambda h: (h, 0, 0, 0)),),
        scratch_shapes=[
            pltpu.VMEM((blocks, ROWS, ROWS), F32),
            pltpu.VMEM((BASE * blocks, ROWS), F32),
            pltpu.VMEM((BASE * blocks, BASE * ROWS), F32),
            pltpu.VMEM((BASE * blocks, ROWS), F32),
            pltpu.VMEM((nodes, DK, DK), F32),
            pltpu.VMEM((nodes, DK, DK), F32),
            pltpu.VMEM((nodes, DK, DK), F32),
        ],
        compiler_params=params(),
        cost_estimate=pl.CostEstimate(
            flops=blocks * 270 * DK**3, bytes_accessed=8 << 20, transcendentals=0
        ),
        name="local_pass",
    )(jnp.asarray(spread_table(), BF), projected, logits, d_out, *marks)


def grad_kernel(
    blocks,
    unroll,
    marks,
    head,
    proj_ref,
    logit_ref,
    grad_ref,
    key_ref,
    inv_ref,
    wide_ref,
    upd_ref,
    read_ref,
    map_ref,
    shift_ref,
    source_ref,
    edge_ref,
    *rest,
):
    out_ref, rate_ref, states, ends = rest[marks:]
    nodes = 2 * blocks - 1
    states[nodes - 1] = edge_ref[0, 0]
    ends[nodes - 1] = edge_ref[0, 1]
    count, offset = 2, nodes - 3
    while count <= blocks:
        pairs = [(offset + 2 * pair, offset + count + pair) for pair in range(count // 2)]
        onward = [nn(map_ref[0, left], states[parent]) for left, parent in pairs]
        backward = [tn(map_ref[0, left + 1], ends[parent]) for left, parent in pairs]
        for (left, parent), ahead, behind in zip(pairs, onward, backward):
            state, end = states[parent], ends[parent]
            states[left] = state
            states[left + 1] = state + ahead + shift_ref[0, left].astype(F32)
            ends[left + 1] = end
            ends[left] = end + behind + source_ref[0, left + 1].astype(F32)
        count *= 2
        offset -= count

    strict = strict_mask()
    visible = visible_mask()

    def body(outer, carry):
        own = [outer * unroll + inner for inner in range(unroll)]
        rows = [pl.ds(pl.multiple_of(block * SPAN, SPAN), SPAN) for block in own]
        state = [states[block].astype(BF) for block in own]
        end = [ends[block].astype(BF) for block in own]
        back = [
            (read_ref[0, block].astype(F32) + nn(key_ref[0, block], e)).astype(BF)
            for block, e in zip(own, end)
        ]
        delta = [
            (upd_ref[0, block].astype(F32) - nn(wide_ref[0, block], s)).astype(BF)
            for block, s in zip(own, state)
        ]
        held = [tn(inv_ref[0, block], b) for block, b in zip(own, back)]
        many = [
            nt(
                jnp.concatenate([grad_ref[r, :], h.astype(BF)], 0),
                jnp.concatenate([d, s], 0),
            )
            for r, h, d, s in zip(rows, held, delta, state)
        ]
        masked = [
            jnp.concatenate(
                [
                    jnp.where(visible, m[:SPAN, :ROWS], 0.0),
                    jnp.where(strict, m[SPAN:, :ROWS], 0.0),
                ],
                0,
            ).astype(BF)
            for m in many
        ]
        onward = [nn(m, key_ref[0, block]) for block, m in zip(own, masked)]
        direct = [nt(d, e) for d, e in zip(delta, end)]
        for inner, (block, r) in enumerate(zip(own, rows)):
            raw = stack_steps(proj_ref, r, 1)
            scale = lax.rsqrt(jnp.sum(raw * raw, axis=1, keepdims=True) + 1e-06)
            keys = raw * scale
            strengths = strengths_of(logit_ref, r, head)
            values = stack_steps(proj_ref, r, 3)
            crossed = tn(
                masked[inner],
                jnp.concatenate([proj_ref[r, 0:DK], (-strengths * keys).astype(BF)], 0),
            )
            d_query = many[inner][:SPAN, ROWS:] + onward[inner][:SPAN]
            inner_sum = many[inner][SPAN:, ROWS:] + onward[inner][SPAN:]
            d_keys = crossed + direct[inner] - strengths * inner_sum
            d_values = strengths * held[inner]
            d_rate = jnp.sum(held[inner] * values - keys * inner_sum, axis=1, keepdims=True)
            d_raw = scale * (d_keys - keys * jnp.sum(keys * d_keys, axis=1, keepdims=True))
            d_logit = d_rate * strengths * (1.0 - 0.5 * strengths)
            out_ref[r, 0:DK] = d_query.astype(BF)
            out_ref[r, DK : 2 * DK] = d_raw[:SPAN].astype(BF)
            out_ref[r, 2 * DK : 3 * DK] = d_raw[SPAN:].astype(BF)
            out_ref[r, 3 * DK : 4 * DK] = d_values[:SPAN].astype(BF)
            out_ref[r, 4 * DK : 5 * DK] = d_values[SPAN:].astype(BF)
            rate_ref[r, :] = jnp.concatenate([d_logit[:SPAN], d_logit[SPAN:]], 1)
        return carry

    lax.fori_loop(0, blocks // unroll, body, 0)


def grad_pass(projected, logits, d_out, kept, edges, head, marks=()):
    tokens = projected.shape[0]
    blocks = tokens // SPAN
    nodes = 2 * blocks - 1
    tile = pl.BlockSpec((1, blocks, ROWS, DK), lambda h: (h, 0, 0, 0))
    branch = pl.BlockSpec((1, nodes, DK, DK), lambda h: (h, 0, 0, 0))
    unroll = divisor(blocks, 4)
    return pl.pallas_call(
        functools.partial(grad_kernel, blocks, unroll, len(marks), head),
        grid=(1,),
        out_shape=(
            jax.ShapeDtypeStruct((tokens, COLS), BF),
            jax.ShapeDtypeStruct((tokens, 2), F32),
        ),
        in_specs=[
            pl.BlockSpec((tokens, COLS), lambda h: (0, h)),
            pl.BlockSpec((tokens, logits.shape[1]), lambda h: (0, 0)),
            pl.BlockSpec((tokens, DK), lambda h: (0, head)),
        ]
        + [tile] * 5
        + [branch] * 3
        + [pl.BlockSpec((1, 2, DK, DK), lambda h: (h, 0, 0, 0))]
        + [pl.BlockSpec(memory_space=pl.ANY)] * len(marks),
        out_specs=(
            pl.BlockSpec((tokens, COLS), lambda h: (0, h)),
            pl.BlockSpec((tokens, 2), lambda h: (0, 0)),
        ),
        scratch_shapes=[
            pltpu.VMEM((nodes, DK, DK), F32),
            pltpu.VMEM((nodes, DK, DK), F32),
        ],
        compiler_params=params(),
        cost_estimate=pl.CostEstimate(
            flops=blocks * 300 * DK**3, bytes_accessed=8 << 20, transcendentals=0
        ),
        name="grad_pass",
    )(projected, logits, d_out, *kept, edges, *marks)


def bmm(a, b):
    return jnp.einsum("hij,hjk->hik", a.astype(BF), b.astype(BF), preferred_element_type=F32)


def bmm_t(a, b):
    return jnp.einsum("hji,hjk->hik", a.astype(BF), b.astype(BF), preferred_element_type=F32)


def shifted(value, by):
    devices = lax.axis_size("seq")
    pairs = [(i, i + by) for i in range(devices) if 0 <= i + by < devices]
    return lax.ppermute(value.astype(BF), "seq", pairs).astype(F32)


def exchange(total):
    devices = lax.axis_size("seq")
    tail_map, tail_shift, head_source = total[:, 0], total[:, 1], total[:, 2]
    head_map = tail_map
    past_map = past_shift = next_map = next_source = None
    by = 1
    while by < devices:
        last = 2 * by >= devices
        if last:
            got_shift = shifted(tail_shift, by)
            got_source = shifted(head_source, -by)
        else:
            behind = shifted(jnp.concatenate([tail_map, tail_shift], 2), by)
            ahead = shifted(jnp.concatenate([head_map, head_source], 2), -by)
            got_map, got_shift = behind[:, :, :DK], behind[:, :, DK:]
            got_next, got_source = ahead[:, :, :DK], ahead[:, :, DK:]
        if past_map is None:
            past_shift, next_source = got_shift, got_source
        else:
            past_shift = past_shift + got_shift + bmm(past_map, got_shift)
            next_source = next_source + got_source + bmm_t(next_map, got_source)
        if not last:
            if past_map is None:
                past_map, next_map = got_map, got_next
            else:
                past_map = past_map + got_map + bmm(past_map, got_map)
                next_map = next_map + got_next + bmm(got_next, next_map)
            tail_shift = tail_shift + got_shift + bmm(tail_map, got_shift)
            head_source = head_source + got_source + bmm_t(head_map, got_source)
            tail_map = tail_map + got_map + bmm(tail_map, got_map)
            head_map = head_map + got_next + bmm(got_next, head_map)
        by *= 2
    return jnp.stack([past_shift, next_source], 1)


def flipped(value, bit):
    devices = lax.axis_size("head")
    return lax.ppermute(value, "head", [(i, i ^ bit) for i in range(devices)])


def line_step(value, stride, count, step, ways):
    pairs = []
    for device in range(lax.axis_size("seq")):
        place = device // stride % count
        for way in ways:
            if 0 <= place + way * step < count:
                pairs.append((device, device + way * stride))
    return lax.ppermute(value.astype(BF), "seq", pairs).astype(F32)


def line_scatter(part, stride, count):
    place = lax.axis_index("seq") // stride % count
    if count == 1:
        return part(place).astype(F32)
    first = part(jnp.where(2 * place < count, count - 1, 0))
    arrived = line_step(first, stride, count, count - 1, (1, -1))
    if count == 2:
        return part(place).astype(F32) + arrived
    total = part(place).astype(F32)
    for way in (1, -1):
        got = jnp.where(place == (1 if way == 1 else count - 2), arrived, 0.0)
        for step in range(count - 2, 0, -1):
            value = part(jnp.clip(place + way * step, 0, count - 1)).astype(F32) + got
            got = line_step(value, stride, count, step, (way,))
        total = total + got
    return total


def side_product(side, grads):
    return lax.dot_general(
        side, grads, (((0,), (0,)), ((), ())), preferred_element_type=F32
    ).astype(BF)


def inner_scatter(sides, grads):
    devices = lax.axis_size("seq")
    inner = sides.shape[0]
    place = lax.axis_index("seq") % inner

    def product(index):
        return side_product(lax.dynamic_index_in_dim(sides, index, 0, keepdims=False), grads)

    if inner == 2:
        leaving = product(1 - place)
        arriving = lax.ppermute(leaving, "seq", [(i, i ^ 1) for i in range(devices)])
        kept = lax.optimization_barrier(product(place))
        return kept, arriving, leaving
    total = line_scatter(product, 1, inner)
    return total, jnp.zeros(total.shape, BF), total


def outer_scatter(total, inner):
    outer = lax.axis_size("seq") // inner
    rows = total.shape[0] // outer
    return line_scatter(
        lambda index: lax.dynamic_slice_in_dim(total, index * rows, rows, 0), inner, outer
    )


def rate_total(part):
    devices = lax.axis_size("seq")
    rows = part.shape[1] // devices
    if devices & (devices - 1):
        return lax.psum_scatter(part.T.astype(BF), "seq", scatter_dimension=0, tiled=True).astype(F32)
    by = 1
    while by < devices:
        got = lax.ppermute(part.astype(BF), "seq", [(i, i ^ by) for i in range(devices)])
        part = part + got.astype(F32)
        by *= 2
    return lax.dynamic_slice_in_dim(part, lax.axis_index("seq") * rows, rows, 1).T


def shards(layer_input, w_proj, w_beta, beta_bias, d_out):
    tokens, features = layer_input.shape
    heads = w_beta.shape[1] // 2
    devices = lax.axis_size("seq")
    spread = lax.axis_size("head")
    columns = [slice(head * COLS, (head + 1) * COLS) for head in range(heads)]
    if spread == 4:
        index = lax.axis_index("head")
        mate = flipped(layer_input, 1)
        far = flipped(layer_input, 2)
        far_mate = flipped(far, 1)
        whole = jnp.zeros((tokens, spread * features), BF)
        for bit, part in enumerate((layer_input, mate, far, far_mate)):
            whole = lax.dynamic_update_slice_in_dim(whole, part, (index ^ bit) * features, 1)
    else:
        whole = lax.all_gather(layer_input, "head", axis=1, tiled=True)
    logits = jnp.dot(whole, w_beta, preferred_element_type=F32) + beta_bias
    projected = [
        jnp.dot(whole, w_proj[:, part], preferred_element_type=F32).astype(BF) for part in columns
    ]
    outer = 4 if devices % 4 == 0 else devices
    inner = devices // outer
    sides = jnp.transpose(
        whole.reshape(tokens, outer, inner, whole.shape[1] // devices), (2, 0, 1, 3)
    ).reshape(inner, tokens, whole.shape[1] // inner)

    kept, totals = [], []
    for head in range(heads):
        *values, total = local_pass(projected[head], logits, d_out, head)
        kept.append(values)
        totals.append(total)
    edges = exchange(jnp.concatenate(totals, 0))
    grads, rates, pieces = [], [], []
    early = (heads + 1) // 2
    wait = []
    for head in range(heads):
        grad, rate = grad_pass(
            projected[head], logits, d_out, kept[head], edges[head : head + 1], head, wait
        )
        grads.append(grad)
        rates.append(rate)
        wait = [rate]
        if head == early - 1:
            sent = side_product(whole, jnp.concatenate(grads, 1))
            weights = [lax.psum_scatter(sent, "seq", scatter_dimension=0, tiled=True).astype(F32)]
            wait = [sent]
        elif head >= early:
            *piece, sent = inner_scatter(sides, grad)
            pieces.append(piece)
            wait = [sent]
    grad_logits = jnp.concatenate(rates, 1).astype(BF)
    grad_beta = rate_total(
        lax.dot_general(
            grad_logits, whole, (((0,), (0,)), ((), ())), preferred_element_type=F32
        )
    )
    grad_projected = jnp.concatenate(grads, 1)

    def input_part(weights, rate_weights):
        return (
            jnp.einsum("tc,dc->td", grad_projected, weights, preferred_element_type=F32)
            + jnp.einsum("tc,dc->td", grad_logits, rate_weights, preferred_element_type=F32)
        ).astype(BF)

    if spread == 4:
        core, chip = index % 2, index // 2

        def rows_of(weights, side):
            parts = weights.reshape(2, 2, features, weights.shape[1])
            return lax.dynamic_index_in_dim(parts, side, 1, keepdims=False).reshape(
                2 * features, weights.shape[1]
            )

        arrived = flipped(input_part(rows_of(w_proj, 1 - core), rows_of(w_beta, 1 - core)), 1)
        own = input_part(rows_of(w_proj, core), rows_of(w_beta, core))
        parts = lax.optimization_barrier(own).astype(F32) + arrived
        leaving = lax.dynamic_slice_in_dim(parts, (1 - chip) * features, features, 1).astype(BF)
        arrived = flipped(leaving, 2)
        grad_input = (
            lax.dynamic_slice_in_dim(parts, chip * features, features, 1) + arrived
        ).astype(BF)
    else:
        grad_input = lax.psum_scatter(
            input_part(w_proj, w_beta), "head", scatter_dimension=1, tiled=True
        )
    for keep, arrived in pieces:
        weights.append(outer_scatter(keep.astype(F32) + arrived, inner))
    return (grad_input, jnp.concatenate(weights, 1), grad_beta)


def solution(mesh):
    in_specs = (P("seq", "head"), P(None, "head"), P(None, "head"), P("head"), P("seq", "head"))
    out_specs = (P("seq", "head"), P("seq", "head"), P("seq", "head"))
    return jax.shard_map(shards, mesh=mesh, in_specs=in_specs, out_specs=out_specs, check_vma=False)
```

```python
import functools

import jax
import jax.numpy as jnp
import numpy as np
from jax import lax
from jax.experimental import pallas as pl
from jax.experimental.pallas import tpu as pltpu
from jax.sharding import PartitionSpec as P

DK = 128
SPAN = 64
ROWS = 2 * SPAN
BASE = 16
HALF = BASE // 2
COLS = 5 * DK
BF = jnp.bfloat16
F32 = jnp.float32
VMEM_LIMIT = 56 << 20


def dot(a, b, ca, cb):
    return lax.dot_general(
        a.astype(BF), b.astype(BF), (((ca,), (cb,)), ((), ())), preferred_element_type=F32
    )


def nn(a, b):
    return dot(a, b, 1, 0)


def nt(a, b):
    return dot(a, b, 1, 1)


def tn(a, b):
    return dot(a, b, 0, 0)


def split(a):
    high = a.astype(BF)
    return high, (a - high.astype(F32)).astype(BF)


def nn3(a, b):
    ah, al = split(a)
    bh, bl = split(b)
    return nn(jnp.concatenate([ah, al], 1), jnp.concatenate([bh, bh], 0)) + nn(ah, bl)


def nt3(a, b):
    ah, al = split(a)
    bh, bl = split(b)
    return nt(jnp.concatenate([ah, al], 1), jnp.concatenate([bh, bh], 1)) + nt(ah, bl)


def rows_cols(rows, cols):
    row = lax.broadcasted_iota(jnp.int32, (rows, cols), 0)
    col = lax.broadcasted_iota(jnp.int32, (rows, cols), 1)
    return row, col


def order(index):
    return 2 * (index % SPAN) + index // SPAN


def strict_mask():
    row, col = rows_cols(ROWS, ROWS)
    return order(col) < order(row)


def visible_mask():
    row, col = rows_cols(SPAN, ROWS)
    return col % SPAN <= row


def stack_steps(ref, rows, first):
    return jnp.concatenate(
        [ref[rows, first * DK : (first + 1) * DK], ref[rows, (first + 1) * DK : (first + 2) * DK]], 0
    ).astype(F32)


def strengths_of(logit_ref, rows, head):
    pair = logit_ref[rows, 2 * head : 2 * head + 2]
    return 2.0 * jax.nn.sigmoid(jnp.concatenate([pair[:, 0:1], pair[:, 1:2]], 0))


def spread_table():
    table = np.zeros((DK, BASE, DK), np.float32)
    for lane in range(DK):
        group = (lane % SPAN) // HALF
        for member in range(BASE):
            source = (member // HALF) * SPAN + group * HALF + member % HALF
            table[source, member, lane] = 1.0
    return table.reshape(DK, BASE * DK)


def local_kernel(
    blocks,
    unroll,
    marks,
    head,
    spread_ref,
    proj_ref,
    logit_ref,
    grad_ref,
    *rest,
):
    (
    key_ref,
    inv_ref,
    wide_ref,
    upd_ref,
    read_ref,
    map_ref,
    shift_ref,
    source_ref,
    total_ref,
    system,
    packed,
    coef,
    solved,
    maps,
    shifts,
    sources,
    ) = rest[marks:]
    strict = strict_mask()
    lane_group = (rows_cols(HALF, ROWS)[1] % SPAN) // HALF

    def first(outer, carry):
        for inner in range(unroll):
            block = outer * unroll + inner
            rows = pl.ds(pl.multiple_of(block * SPAN, SPAN), SPAN)
            raw = stack_steps(proj_ref, rows, 1)
            strengths = strengths_of(logit_ref, rows, head)
            keys = raw * lax.rsqrt(jnp.sum(raw * raw, axis=1, keepdims=True) + 1e-06)
            key_ref[0, block] = keys.astype(BF)
            lower = jnp.where(strict, strengths * nt3(keys, keys), 0.0)
            system[block] = lower
            for step in range(2):
                piece = jnp.zeros((HALF, ROWS), F32)
                for group in range(SPAN // HALF):
                    start = step * SPAN + group * HALF
                    piece = jnp.where(lane_group == group, lower[start : start + HALF], piece)
                packed[pl.ds(step * HALF * blocks + block, HALF, stride=blocks), :] = piece
        return carry

    lax.fori_loop(0, blocks // unroll, first, 0)

    high, low = split(packed[...])
    spread = spread_ref[...]
    coef[...] = nn(jnp.concatenate([high, low], 1), jnp.concatenate([spread, spread], 0))
    lane = rows_cols(blocks, ROWS)[1]
    found = {}
    for when in range(BASE):
        step, tick = when % 2, when // 2
        here = step * HALF + tick
        value = jnp.where((lane // SPAN == step) & (lane % HALF == tick), 1.0, 0.0)
        for before in range(when):
            there = (before % 2) * HALF + before // 2
            weight = coef[here * blocks : (here + 1) * blocks, there * ROWS : (there + 1) * ROWS]
            value = value - weight * found[before]
        found[when] = value
        solved[here * blocks : (here + 1) * blocks, :] = value

    row, col = rows_cols(ROWS, ROWS)
    row_time, col_time = order(row), order(col)
    visible = visible_mask()

    joins = []
    size = BASE
    while size < ROWS:
        joins.append(
            (row_time // (2 * size) == col_time // (2 * size))
            & (row_time // size != col_time // size)
        )
        size *= 2

    def second(outer, carry):
        own = [outer * unroll + inner for inner in range(unroll)]
        rows = [pl.ds(pl.multiple_of(block * SPAN, SPAN), SPAN) for block in own]
        inverse = []
        for block in own:
            pieces = []
            for step in range(2):
                piece = solved[pl.ds(step * HALF * blocks + block, HALF, stride=blocks), :]
                for group in range(SPAN // HALF):
                    pieces.append(jnp.where(lane_group == group, piece, 0.0))
            inverse.append(jnp.concatenate(pieces, 0))
        for join in joins:
            half = [
                nn3(jnp.where(join, system[block], 0.0), inv) for block, inv in zip(own, inverse)
            ]
            inverse = [inv - nn3(inv, x) for inv, x in zip(inverse, half)]
        inverse = [inv.astype(BF) for inv in inverse]
        scores = [
            jnp.where(visible, nt(proj_ref[r, 0:DK], key_ref[0, block]), 0.0).astype(BF)
            for block, r in zip(own, rows)
        ]
        reads = [tn(score, grad_ref[r, :]).astype(BF) for score, r in zip(scores, rows)]
        both = []
        for block, r, inv in zip(own, rows, inverse):
            inv_ref[0, block] = inv
            strengths = strengths_of(logit_ref, r, head)
            keys = key_ref[0, block].astype(F32)
            values = stack_steps(proj_ref, r, 3)
            targets = jnp.concatenate([strengths * keys, strengths * values], 1)
            both.append(nn(inv, targets).astype(BF))
        folded = [tn(key_ref[0, block], x) for block, x in zip(own, both)]
        gained = [
            tn(proj_ref[r, 0:DK], grad_ref[r, :]) - tn(x[:, :DK], read)
            for r, x, read in zip(rows, both, reads)
        ]
        for block, x, read, fold, gain in zip(own, both, reads, folded, gained):
            wide_ref[0, block] = x[:, :DK]
            upd_ref[0, block] = x[:, DK:]
            read_ref[0, block] = read
            maps[block] = -fold[:, :DK]
            shifts[block] = fold[:, DK:]
            sources[block] = gain
        return carry

    lax.fori_loop(0, blocks // unroll, second, 0)

    offset, count = 0, blocks
    while count > 1:
        half = count // 2
        lefts = [offset + 2 * pair for pair in range(half)]
        joined = [
            nn(maps[left + 1], jnp.concatenate([maps[left], shifts[left]], 1)) for left in lefts
        ]
        moved = [tn(maps[left], sources[left + 1]) for left in lefts]
        for pair, left in enumerate(lefts):
            parent = offset + count + pair
            maps[parent] = maps[left] + maps[left + 1] + joined[pair][:, :DK]
            shifts[parent] = shifts[left] + shifts[left + 1] + joined[pair][:, DK:]
            sources[parent] = sources[left] + sources[left + 1] + moved[pair]
        offset += count
        count //= 2
    map_ref[0] = maps[...].astype(BF)
    shift_ref[0] = shifts[...].astype(BF)
    source_ref[0] = sources[...].astype(BF)
    total_ref[0, 0] = maps[offset]
    total_ref[0, 1] = shifts[offset]
    total_ref[0, 2] = sources[offset]


def divisor(blocks, most):
    while blocks % most:
        most //= 2
    return most


def params():
    return pltpu.CompilerParams(
        dimension_semantics=("arbitrary",), vmem_limit_bytes=VMEM_LIMIT
    )


def local_pass(projected, logits, d_out, head, marks=()):
    tokens = projected.shape[0]
    blocks = tokens // SPAN
    nodes = 2 * blocks - 1
    square = jax.ShapeDtypeStruct((1, blocks, ROWS, DK), BF)
    tree = jax.ShapeDtypeStruct((1, nodes, DK, DK), BF)
    tile = pl.BlockSpec((1, blocks, ROWS, DK), lambda h: (h, 0, 0, 0))
    branch = pl.BlockSpec((1, nodes, DK, DK), lambda h: (h, 0, 0, 0))
    unroll = divisor(blocks, 16)
    return pl.pallas_call(
        functools.partial(local_kernel, blocks, unroll, len(marks), head),
        grid=(1,),
        out_shape=(square,) * 5
        + (tree,) * 3
        + (jax.ShapeDtypeStruct((1, 3, DK, DK), F32),),
        in_specs=[
            pl.BlockSpec((DK, BASE * DK), lambda h: (0, 0)),
            pl.BlockSpec((tokens, COLS), lambda h: (0, h)),
            pl.BlockSpec((tokens, logits.shape[1]), lambda h: (0, 0)),
            pl.BlockSpec((tokens, DK), lambda h: (0, head)),
        ]
        + [pl.BlockSpec(memory_space=pl.ANY)] * len(marks),
        out_specs=(tile,) * 5
        + (branch,) * 3
        + (pl.BlockSpec((1, 3, DK, DK), lambda h: (h, 0, 0, 0)),),
        scratch_shapes=[
            pltpu.VMEM((blocks, ROWS, ROWS), F32),
            pltpu.VMEM((BASE * blocks, ROWS), F32),
            pltpu.VMEM((BASE * blocks, BASE * ROWS), F32),
            pltpu.VMEM((BASE * blocks, ROWS), F32),
            pltpu.VMEM((nodes, DK, DK), F32),
            pltpu.VMEM((nodes, DK, DK), F32),
            pltpu.VMEM((nodes, DK, DK), F32),
        ],
        compiler_params=params(),
        cost_estimate=pl.CostEstimate(
            flops=blocks * 270 * DK**3, bytes_accessed=8 << 20, transcendentals=0
        ),
        name="local_pass",
    )(jnp.asarray(spread_table(), BF), projected, logits, d_out, *marks)


def grad_kernel(
    blocks,
    unroll,
    marks,
    head,
    proj_ref,
    logit_ref,
    grad_ref,
    key_ref,
    inv_ref,
    wide_ref,
    upd_ref,
    read_ref,
    map_ref,
    shift_ref,
    source_ref,
    edge_ref,
    *rest,
):
    out_ref, rate_ref, states, ends = rest[marks:]
    nodes = 2 * blocks - 1
    states[nodes - 1] = edge_ref[0, 0]
    ends[nodes - 1] = edge_ref[0, 1]
    count, offset = 2, nodes - 3
    while count <= blocks:
        pairs = [(offset + 2 * pair, offset + count + pair) for pair in range(count // 2)]
        onward = [nn(map_ref[0, left], states[parent]) for left, parent in pairs]
        backward = [tn(map_ref[0, left + 1], ends[parent]) for left, parent in pairs]
        for (left, parent), ahead, behind in zip(pairs, onward, backward):
            state, end = states[parent], ends[parent]
            states[left] = state
            states[left + 1] = state + ahead + shift_ref[0, left].astype(F32)
            ends[left + 1] = end
            ends[left] = end + behind + source_ref[0, left + 1].astype(F32)
        count *= 2
        offset -= count

    strict = strict_mask()
    visible = visible_mask()

    def body(outer, carry):
        own = [outer * unroll + inner for inner in range(unroll)]
        rows = [pl.ds(pl.multiple_of(block * SPAN, SPAN), SPAN) for block in own]
        state = [states[block].astype(BF) for block in own]
        end = [ends[block].astype(BF) for block in own]
        back = [
            (read_ref[0, block].astype(F32) + nn(key_ref[0, block], e)).astype(BF)
            for block, e in zip(own, end)
        ]
        delta = [
            (upd_ref[0, block].astype(F32) - nn(wide_ref[0, block], s)).astype(BF)
            for block, s in zip(own, state)
        ]
        held = [tn(inv_ref[0, block], b) for block, b in zip(own, back)]
        many = [
            nt(
                jnp.concatenate([grad_ref[r, :], h.astype(BF)], 0),
                jnp.concatenate([d, s], 0),
            )
            for r, h, d, s in zip(rows, held, delta, state)
        ]
        masked = [
            jnp.concatenate(
                [
                    jnp.where(visible, m[:SPAN, :ROWS], 0.0),
                    jnp.where(strict, m[SPAN:, :ROWS], 0.0),
                ],
                0,
            ).astype(BF)
            for m in many
        ]
        onward = [nn(m, key_ref[0, block]) for block, m in zip(own, masked)]
        direct = [nt(d, e) for d, e in zip(delta, end)]
        for inner, (block, r) in enumerate(zip(own, rows)):
            raw = stack_steps(proj_ref, r, 1)
            scale = lax.rsqrt(jnp.sum(raw * raw, axis=1, keepdims=True) + 1e-06)
            keys = raw * scale
            strengths = strengths_of(logit_ref, r, head)
            values = stack_steps(proj_ref, r, 3)
            crossed = tn(
                masked[inner],
                jnp.concatenate([proj_ref[r, 0:DK], (-strengths * keys).astype(BF)], 0),
            )
            d_query = many[inner][:SPAN, ROWS:] + onward[inner][:SPAN]
            inner_sum = many[inner][SPAN:, ROWS:] + onward[inner][SPAN:]
            d_keys = crossed + direct[inner] - strengths * inner_sum
            d_values = strengths * held[inner]
            d_rate = jnp.sum(held[inner] * values - keys * inner_sum, axis=1, keepdims=True)
            d_raw = scale * (d_keys - keys * jnp.sum(keys * d_keys, axis=1, keepdims=True))
            d_logit = d_rate * strengths * (1.0 - 0.5 * strengths)
            out_ref[r, 0:DK] = d_query.astype(BF)
            out_ref[r, DK : 2 * DK] = d_raw[:SPAN].astype(BF)
            out_ref[r, 2 * DK : 3 * DK] = d_raw[SPAN:].astype(BF)
            out_ref[r, 3 * DK : 4 * DK] = d_values[:SPAN].astype(BF)
            out_ref[r, 4 * DK : 5 * DK] = d_values[SPAN:].astype(BF)
            rate_ref[r, :] = jnp.concatenate([d_logit[:SPAN], d_logit[SPAN:]], 1)
        return carry

    lax.fori_loop(0, blocks // unroll, body, 0)


def grad_pass(projected, logits, d_out, kept, edges, head, marks=()):
    tokens = projected.shape[0]
    blocks = tokens // SPAN
    nodes = 2 * blocks - 1
    tile = pl.BlockSpec((1, blocks, ROWS, DK), lambda h: (h, 0, 0, 0))
    branch = pl.BlockSpec((1, nodes, DK, DK), lambda h: (h, 0, 0, 0))
    unroll = divisor(blocks, 4)
    return pl.pallas_call(
        functools.partial(grad_kernel, blocks, unroll, len(marks), head),
        grid=(1,),
        out_shape=(
            jax.ShapeDtypeStruct((tokens, COLS), BF),
            jax.ShapeDtypeStruct((tokens, 2), F32),
        ),
        in_specs=[
            pl.BlockSpec((tokens, COLS), lambda h: (0, h)),
            pl.BlockSpec((tokens, logits.shape[1]), lambda h: (0, 0)),
            pl.BlockSpec((tokens, DK), lambda h: (0, head)),
        ]
        + [tile] * 5
        + [branch] * 3
        + [pl.BlockSpec((1, 2, DK, DK), lambda h: (h, 0, 0, 0))]
        + [pl.BlockSpec(memory_space=pl.ANY)] * len(marks),
        out_specs=(
            pl.BlockSpec((tokens, COLS), lambda h: (0, h)),
            pl.BlockSpec((tokens, 2), lambda h: (0, 0)),
        ),
        scratch_shapes=[
            pltpu.VMEM((nodes, DK, DK), F32),
            pltpu.VMEM((nodes, DK, DK), F32),
        ],
        compiler_params=params(),
        cost_estimate=pl.CostEstimate(
            flops=blocks * 300 * DK**3, bytes_accessed=8 << 20, transcendentals=0
        ),
        name="grad_pass",
    )(projected, logits, d_out, *kept, edges, *marks)


def bmm(a, b):
    return jnp.einsum("hij,hjk->hik", a.astype(BF), b.astype(BF), preferred_element_type=F32)


def bmm_t(a, b):
    return jnp.einsum("hji,hjk->hik", a.astype(BF), b.astype(BF), preferred_element_type=F32)


def shifted(value, by):
    devices = lax.axis_size("seq")
    pairs = [(i, i + by) for i in range(devices) if 0 <= i + by < devices]
    return lax.ppermute(value.astype(BF), "seq", pairs).astype(F32)


def exchange(total):
    devices = lax.axis_size("seq")
    tail_map, tail_shift, head_source = total[:, 0], total[:, 1], total[:, 2]
    head_map = tail_map
    past_map = past_shift = next_map = next_source = None
    by = 1
    while by < devices:
        last = 2 * by >= devices
        if last:
            got_shift = shifted(tail_shift, by)
            got_source = shifted(head_source, -by)
        else:
            behind = shifted(jnp.concatenate([tail_map, tail_shift], 2), by)
            ahead = shifted(jnp.concatenate([head_map, head_source], 2), -by)
            got_map, got_shift = behind[:, :, :DK], behind[:, :, DK:]
            got_next, got_source = ahead[:, :, :DK], ahead[:, :, DK:]
        if past_map is None:
            past_shift, next_source = got_shift, got_source
        else:
            past_shift = past_shift + got_shift + bmm(past_map, got_shift)
            next_source = next_source + got_source + bmm_t(next_map, got_source)
        if not last:
            if past_map is None:
                past_map, next_map = got_map, got_next
            else:
                past_map = past_map + got_map + bmm(past_map, got_map)
                next_map = next_map + got_next + bmm(got_next, next_map)
            tail_shift = tail_shift + got_shift + bmm(tail_map, got_shift)
            head_source = head_source + got_source + bmm_t(head_map, got_source)
            tail_map = tail_map + got_map + bmm(tail_map, got_map)
            head_map = head_map + got_next + bmm(got_next, head_map)
        by *= 2
    return jnp.stack([past_shift, next_source], 1)


def flipped(value, bit):
    devices = lax.axis_size("head")
    return lax.ppermute(value, "head", [(i, i ^ bit) for i in range(devices)])


def line_step(value, stride, count, step, ways):
    pairs = []
    for device in range(lax.axis_size("seq")):
        place = device // stride % count
        for way in ways:
            if 0 <= place + way * step < count:
                pairs.append((device, device + way * stride))
    return lax.ppermute(value.astype(BF), "seq", pairs)


def line_scatter(part, stride, count):
    place = lax.axis_index("seq") // stride % count
    if count == 1:
        return part(place).astype(F32), []
    first = part(jnp.where(2 * place < count, count - 1, 0))
    arrived = line_step(first, stride, count, count - 1, (1, -1))
    if count == 2:
        return part(place).astype(F32) + arrived.astype(F32), [arrived]
    held = {}
    for way in (1, -1):
        held[way] = jnp.where(place == (1 if way == 1 else count - 2), arrived.astype(F32), 0.0)
    for step in range(count - 2, 0, -1):
        came = []
        for way in (1, -1):
            value = part(jnp.clip(place + way * step, 0, count - 1)).astype(F32) + held[way]
            came.append(line_step(value, stride, count, step, (way,)))
            held[way] = came[-1].astype(F32)
        if step == 2:
            before = came
    return part(place).astype(F32) + held[1] + held[-1], before if count > 3 else [arrived]


def side_product(side, grads):
    return lax.dot_general(
        side, grads, (((0,), (0,)), ((), ())), preferred_element_type=F32
    ).astype(BF)


def inner_scatter(sides, grads):
    devices = lax.axis_size("seq")
    inner = sides.shape[0]
    place = lax.axis_index("seq") % inner

    def product(index):
        return side_product(lax.dynamic_index_in_dim(sides, index, 0, keepdims=False), grads)

    if inner == 2:
        leaving = product(1 - place)
        arriving = lax.ppermute(leaving, "seq", [(i, i ^ 1) for i in range(devices)])
        kept = lax.optimization_barrier(product(place))
        return kept, arriving, leaving
    total, unused = line_scatter(product, 1, inner)
    return total, jnp.zeros(total.shape, BF), total


def outer_scatter(total, inner):
    outer = lax.axis_size("seq") // inner
    rows = total.shape[0] // outer
    return line_scatter(
        lambda index: lax.dynamic_slice_in_dim(total, index * rows, rows, 0), inner, outer
    )


def rate_total(part):
    devices = lax.axis_size("seq")
    rows = part.shape[1] // devices
    if devices & (devices - 1):
        return lax.psum_scatter(part.T.astype(BF), "seq", scatter_dimension=0, tiled=True).astype(F32)
    by = 1
    while by < devices:
        got = lax.ppermute(part.astype(BF), "seq", [(i, i ^ by) for i in range(devices)])
        part = part + got.astype(F32)
        by *= 2
    return lax.dynamic_slice_in_dim(part, lax.axis_index("seq") * rows, rows, 1).T


def shards(layer_input, w_proj, w_beta, beta_bias, d_out):
    tokens, features = layer_input.shape
    heads = w_beta.shape[1] // 2
    devices = lax.axis_size("seq")
    spread = lax.axis_size("head")
    columns = [slice(head * COLS, (head + 1) * COLS) for head in range(heads)]
    if spread == 4:
        index = lax.axis_index("head")
        mate = flipped(layer_input, 1)
        far = flipped(layer_input, 2)
        far_mate = flipped(far, 1)
        whole = jnp.zeros((tokens, spread * features), BF)
        for bit, part in enumerate((layer_input, mate, far, far_mate)):
            whole = lax.dynamic_update_slice_in_dim(whole, part, (index ^ bit) * features, 1)
    else:
        whole = lax.all_gather(layer_input, "head", axis=1, tiled=True)
    logits = jnp.dot(whole, w_beta, preferred_element_type=F32) + beta_bias
    projected = [
        jnp.dot(whole, w_proj[:, part], preferred_element_type=F32).astype(BF) for part in columns
    ]
    outer = 4 if devices % 4 == 0 else devices
    inner = devices // outer
    sides = jnp.transpose(
        whole.reshape(tokens, outer, inner, whole.shape[1] // devices), (2, 0, 1, 3)
    ).reshape(inner, tokens, whole.shape[1] // inner)

    kept, totals = [], []
    for head in range(heads):
        *values, total = local_pass(projected[head], logits, d_out, head)
        kept.append(values)
        totals.append(total)
    edges = exchange(jnp.concatenate(totals, 0))
    grads, rates, pieces = [], [], []
    early = (heads + 1) // 2
    wait = []
    for head in range(heads):
        grad, rate = grad_pass(
            projected[head], logits, d_out, kept[head], edges[head : head + 1], head, wait
        )
        grads.append(grad)
        rates.append(rate)
        wait = [rate]
        if head == early - 1:
            sent = side_product(whole, jnp.concatenate(grads, 1))
            weights = [lax.psum_scatter(sent, "seq", scatter_dimension=0, tiled=True).astype(F32)]
            wait = [sent]
        elif early <= head < heads - 1:
            *piece, sent = inner_scatter(sides, grad)
            pieces.append(piece)
            wait = [sent]
    grad_logits = jnp.concatenate(rates, 1).astype(BF)
    grad_beta = rate_total(
        lax.dot_general(
            grad_logits, whole, (((0,), (0,)), ((), ())), preferred_element_type=F32
        )
    )
    grad_projected = jnp.concatenate(grads, 1)

    def input_part(weights, rate_weights):
        return (
            jnp.einsum("tc,dc->td", grad_projected, weights, preferred_element_type=F32)
            + jnp.einsum("tc,dc->td", grad_logits, rate_weights, preferred_element_type=F32)
        ).astype(BF)

    if spread == 4:
        core, chip = index % 2, index // 2

        def rows_of(weights, side):
            parts = weights.reshape(2, 2, features, weights.shape[1])
            return lax.dynamic_index_in_dim(parts, side, 1, keepdims=False).reshape(
                2 * features, weights.shape[1]
            )

        arrived = flipped(input_part(rows_of(w_proj, 1 - core), rows_of(w_beta, 1 - core)), 1)
        own = input_part(rows_of(w_proj, core), rows_of(w_beta, core))
        parts = lax.optimization_barrier(own).astype(F32) + arrived
        leaving = lax.dynamic_slice_in_dim(parts, (1 - chip) * features, features, 1).astype(BF)
        arrived = flipped(leaving, 2)
        grad_input = (
            lax.dynamic_slice_in_dim(parts, chip * features, features, 1) + arrived
        ).astype(BF)
    else:
        grad_input = lax.psum_scatter(
            input_part(w_proj, w_beta), "head", scatter_dimension=1, tiled=True
        )
    for keep, arrived in pieces:
        total, unused = outer_scatter(keep.astype(F32) + arrived.astype(F32), inner)
        weights.append(total)
    if heads > 1:
        total, unused = outer_scatter(side_product(whole, grads[-1]), inner)
        rows = total.shape[0] // inner
        total, unused = line_scatter(
            lambda place: lax.dynamic_slice_in_dim(total, place * rows, rows, 0), 1, inner
        )
        weights.append(total)
    return (grad_input, jnp.concatenate(weights, 1), grad_beta)


def solution(mesh):
    in_specs = (P("seq", "head"), P(None, "head"), P(None, "head"), P("head"), P("seq", "head"))
    out_specs = (P("seq", "head"), P("seq", "head"), P("seq", "head"))
    return jax.shard_map(shards, mesh=mesh, in_specs=in_specs, out_specs=out_specs, check_vma=False)
```

```python
import functools

import jax
import jax.numpy as jnp
import numpy as np
from jax import lax
from jax.experimental import pallas as pl
from jax.experimental.pallas import tpu as pltpu
from jax.sharding import PartitionSpec as P

DK = 128
SPAN = 64
ROWS = 2 * SPAN
BASE = 16
HALF = BASE // 2
COLS = 5 * DK
BF = jnp.bfloat16
F32 = jnp.float32
VMEM_LIMIT = 56 << 20


def dot(a, b, ca, cb):
    return lax.dot_general(
        a.astype(BF), b.astype(BF), (((ca,), (cb,)), ((), ())), preferred_element_type=F32
    )


def nn(a, b):
    return dot(a, b, 1, 0)


def nt(a, b):
    return dot(a, b, 1, 1)


def tn(a, b):
    return dot(a, b, 0, 0)


def split(a):
    high = a.astype(BF)
    return high, (a - high.astype(F32)).astype(BF)


def nn3(a, b):
    ah, al = split(a)
    bh, bl = split(b)
    return nn(jnp.concatenate([ah, al], 1), jnp.concatenate([bh, bh], 0)) + nn(ah, bl)


def nt3(a, b):
    ah, al = split(a)
    bh, bl = split(b)
    return nt(jnp.concatenate([ah, al], 1), jnp.concatenate([bh, bh], 1)) + nt(ah, bl)


def rows_cols(rows, cols):
    row = lax.broadcasted_iota(jnp.int32, (rows, cols), 0)
    col = lax.broadcasted_iota(jnp.int32, (rows, cols), 1)
    return row, col


def order(index):
    return 2 * (index % SPAN) + index // SPAN


def strict_mask():
    row, col = rows_cols(ROWS, ROWS)
    return order(col) < order(row)


def visible_mask():
    row, col = rows_cols(SPAN, ROWS)
    return col % SPAN <= row


def stack_steps(ref, rows, first):
    return jnp.concatenate(
        [ref[rows, first * DK : (first + 1) * DK], ref[rows, (first + 1) * DK : (first + 2) * DK]], 0
    ).astype(F32)


def strengths_of(logit_ref, rows, head):
    pair = logit_ref[rows, 2 * head : 2 * head + 2]
    return 2.0 * jax.nn.sigmoid(jnp.concatenate([pair[:, 0:1], pair[:, 1:2]], 0))


def spread_table():
    table = np.zeros((DK, BASE, DK), np.float32)
    for lane in range(DK):
        group = (lane % SPAN) // HALF
        for member in range(BASE):
            source = (member // HALF) * SPAN + group * HALF + member % HALF
            table[source, member, lane] = 1.0
    return table.reshape(DK, BASE * DK)


def local_kernel(
    blocks,
    unroll,
    heads,
    spread_ref,
    proj_ref,
    logit_ref,
    grad_ref,
    key_ref,
    inv_ref,
    wide_ref,
    upd_ref,
    read_ref,
    map_ref,
    shift_ref,
    source_ref,
    total_ref,
    system,
    packed,
    coef,
    solved,
    maps,
    shifts,
    sources,
    rates,
):
    for head in range(heads):

        @pl.when(pl.program_id(0) == head)
        def take(head=head):
            rates[...] = logit_ref[:, 2 * head : 2 * head + 2]

    strict = strict_mask()
    lane_group = (rows_cols(HALF, ROWS)[1] % SPAN) // HALF

    def first(outer, carry):
        for inner in range(unroll):
            block = outer * unroll + inner
            rows = pl.ds(pl.multiple_of(block * SPAN, SPAN), SPAN)
            raw = stack_steps(proj_ref, rows, 1)
            strengths = strengths_of(rates, rows, 0)
            keys = raw * lax.rsqrt(jnp.sum(raw * raw, axis=1, keepdims=True) + 1e-06)
            key_ref[0, block] = keys.astype(BF)
            lower = jnp.where(strict, strengths * nt3(keys, keys), 0.0)
            system[block] = lower
            for step in range(2):
                piece = jnp.zeros((HALF, ROWS), F32)
                for group in range(SPAN // HALF):
                    start = step * SPAN + group * HALF
                    piece = jnp.where(lane_group == group, lower[start : start + HALF], piece)
                packed[pl.ds(step * HALF * blocks + block, HALF, stride=blocks), :] = piece
        return carry

    lax.fori_loop(0, blocks // unroll, first, 0)

    high, low = split(packed[...])
    spread = spread_ref[...]
    coef[...] = nn(jnp.concatenate([high, low], 1), jnp.concatenate([spread, spread], 0))
    lane = rows_cols(blocks, ROWS)[1]
    found = {}
    for when in range(BASE):
        step, tick = when % 2, when // 2
        here = step * HALF + tick
        value = jnp.where((lane // SPAN == step) & (lane % HALF == tick), 1.0, 0.0)
        for before in range(when):
            there = (before % 2) * HALF + before // 2
            weight = coef[here * blocks : (here + 1) * blocks, there * ROWS : (there + 1) * ROWS]
            value = value - weight * found[before]
        found[when] = value
        solved[here * blocks : (here + 1) * blocks, :] = value

    row, col = rows_cols(ROWS, ROWS)
    row_time, col_time = order(row), order(col)
    visible = visible_mask()

    joins = []
    size = BASE
    while size < ROWS:
        joins.append(
            (row_time // (2 * size) == col_time // (2 * size))
            & (row_time // size != col_time // size)
        )
        size *= 2

    def second(outer, carry):
        own = [outer * unroll + inner for inner in range(unroll)]
        rows = [pl.ds(pl.multiple_of(block * SPAN, SPAN), SPAN) for block in own]
        inverse = []
        for block in own:
            pieces = []
            for step in range(2):
                piece = solved[pl.ds(step * HALF * blocks + block, HALF, stride=blocks), :]
                for group in range(SPAN // HALF):
                    pieces.append(jnp.where(lane_group == group, piece, 0.0))
            inverse.append(jnp.concatenate(pieces, 0))
        for join in joins:
            half = [
                nn3(jnp.where(join, system[block], 0.0), inv) for block, inv in zip(own, inverse)
            ]
            inverse = [inv - nn3(inv, x) for inv, x in zip(inverse, half)]
        inverse = [inv.astype(BF) for inv in inverse]
        scores = [
            jnp.where(visible, nt(proj_ref[r, 0:DK], key_ref[0, block]), 0.0).astype(BF)
            for block, r in zip(own, rows)
        ]
        reads = [tn(score, grad_ref[r, :]).astype(BF) for score, r in zip(scores, rows)]
        both = []
        for block, r, inv in zip(own, rows, inverse):
            inv_ref[0, block] = inv
            strengths = strengths_of(rates, r, 0)
            keys = key_ref[0, block].astype(F32)
            values = stack_steps(proj_ref, r, 3)
            targets = jnp.concatenate([strengths * keys, strengths * values], 1)
            both.append(nn(inv, targets).astype(BF))
        folded = [tn(key_ref[0, block], x) for block, x in zip(own, both)]
        gained = [
            tn(proj_ref[r, 0:DK], grad_ref[r, :]) - tn(x[:, :DK], read)
            for r, x, read in zip(rows, both, reads)
        ]
        for block, x, read, fold, gain in zip(own, both, reads, folded, gained):
            wide_ref[0, block] = x[:, :DK]
            upd_ref[0, block] = x[:, DK:]
            read_ref[0, block] = read
            maps[block] = -fold[:, :DK]
            shifts[block] = fold[:, DK:]
            sources[block] = gain
        return carry

    lax.fori_loop(0, blocks // unroll, second, 0)

    offset, count = 0, blocks
    while count > 1:
        half = count // 2
        lefts = [offset + 2 * pair for pair in range(half)]
        joined = [
            nn(maps[left + 1], jnp.concatenate([maps[left], shifts[left]], 1)) for left in lefts
        ]
        moved = [tn(maps[left], sources[left + 1]) for left in lefts]
        for pair, left in enumerate(lefts):
            parent = offset + count + pair
            maps[parent] = maps[left] + maps[left + 1] + joined[pair][:, :DK]
            shifts[parent] = shifts[left] + shifts[left + 1] + joined[pair][:, DK:]
            sources[parent] = sources[left] + sources[left + 1] + moved[pair]
        offset += count
        count //= 2
    map_ref[0] = maps[...].astype(BF)
    shift_ref[0] = shifts[...].astype(BF)
    source_ref[0] = sources[...].astype(BF)
    total_ref[0, 0] = maps[offset]
    total_ref[0, 1] = shifts[offset]
    total_ref[0, 2] = sources[offset]


def divisor(blocks, most):
    while blocks % most:
        most //= 2
    return most


def params():
    return pltpu.CompilerParams(
        dimension_semantics=("arbitrary",), vmem_limit_bytes=VMEM_LIMIT
    )


def local_pass(projected, logits, d_out, heads):
    tokens = projected.shape[0]
    blocks = tokens // SPAN
    nodes = 2 * blocks - 1
    square = jax.ShapeDtypeStruct((heads, blocks, ROWS, DK), BF)
    tree = jax.ShapeDtypeStruct((heads, nodes, DK, DK), BF)
    tile = pl.BlockSpec((1, blocks, ROWS, DK), lambda h: (h, 0, 0, 0))
    branch = pl.BlockSpec((1, nodes, DK, DK), lambda h: (h, 0, 0, 0))
    unroll = divisor(blocks, 16)
    return pl.pallas_call(
        functools.partial(local_kernel, blocks, unroll, heads),
        grid=(heads,),
        out_shape=(square,) * 5
        + (tree,) * 3
        + (jax.ShapeDtypeStruct((heads, 3, DK, DK), F32),),
        in_specs=[
            pl.BlockSpec((DK, BASE * DK), lambda h: (0, 0)),
            pl.BlockSpec((tokens, COLS), lambda h: (0, h)),
            pl.BlockSpec((tokens, logits.shape[1]), lambda h: (0, 0)),
            pl.BlockSpec((tokens, DK), lambda h: (0, h)),
        ],
        out_specs=(tile,) * 5
        + (branch,) * 3
        + (pl.BlockSpec((1, 3, DK, DK), lambda h: (h, 0, 0, 0)),),
        scratch_shapes=[
            pltpu.VMEM((blocks, ROWS, ROWS), F32),
            pltpu.VMEM((BASE * blocks, ROWS), F32),
            pltpu.VMEM((BASE * blocks, BASE * ROWS), F32),
            pltpu.VMEM((BASE * blocks, ROWS), F32),
            pltpu.VMEM((nodes, DK, DK), F32),
            pltpu.VMEM((nodes, DK, DK), F32),
            pltpu.VMEM((nodes, DK, DK), F32),
            pltpu.VMEM((tokens, 2), F32),
        ],
        compiler_params=params(),
        cost_estimate=pl.CostEstimate(
            flops=heads * blocks * 270 * DK**3, bytes_accessed=heads * 8 << 20, transcendentals=0
        ),
        name="local_pass",
    )(jnp.asarray(spread_table(), BF), projected, logits, d_out)


def grad_kernel(
    blocks,
    unroll,
    marks,
    head,
    proj_ref,
    logit_ref,
    grad_ref,
    key_ref,
    inv_ref,
    wide_ref,
    upd_ref,
    read_ref,
    map_ref,
    shift_ref,
    source_ref,
    edge_ref,
    *rest,
):
    out_ref, rate_ref, states, ends = rest[marks:]
    nodes = 2 * blocks - 1
    states[nodes - 1] = edge_ref[0, 0]
    ends[nodes - 1] = edge_ref[0, 1]
    count, offset = 2, nodes - 3
    while count <= blocks:
        pairs = [(offset + 2 * pair, offset + count + pair) for pair in range(count // 2)]
        onward = [nn(map_ref[0, left], states[parent]) for left, parent in pairs]
        backward = [tn(map_ref[0, left + 1], ends[parent]) for left, parent in pairs]
        for (left, parent), ahead, behind in zip(pairs, onward, backward):
            state, end = states[parent], ends[parent]
            states[left] = state
            states[left + 1] = state + ahead + shift_ref[0, left].astype(F32)
            ends[left + 1] = end
            ends[left] = end + behind + source_ref[0, left + 1].astype(F32)
        count *= 2
        offset -= count

    strict = strict_mask()
    visible = visible_mask()

    def body(outer, carry):
        own = [outer * unroll + inner for inner in range(unroll)]
        rows = [pl.ds(pl.multiple_of(block * SPAN, SPAN), SPAN) for block in own]
        state = [states[block].astype(BF) for block in own]
        end = [ends[block].astype(BF) for block in own]
        back = [
            (read_ref[0, block].astype(F32) + nn(key_ref[0, block], e)).astype(BF)
            for block, e in zip(own, end)
        ]
        delta = [
            (upd_ref[0, block].astype(F32) - nn(wide_ref[0, block], s)).astype(BF)
            for block, s in zip(own, state)
        ]
        held = [tn(inv_ref[0, block], b) for block, b in zip(own, back)]
        many = [
            nt(
                jnp.concatenate([grad_ref[r, :], h.astype(BF)], 0),
                jnp.concatenate([d, s], 0),
            )
            for r, h, d, s in zip(rows, held, delta, state)
        ]
        masked = [
            jnp.concatenate(
                [
                    jnp.where(visible, m[:SPAN, :ROWS], 0.0),
                    jnp.where(strict, m[SPAN:, :ROWS], 0.0),
                ],
                0,
            ).astype(BF)
            for m in many
        ]
        onward = [nn(m, key_ref[0, block]) for block, m in zip(own, masked)]
        direct = [nt(d, e) for d, e in zip(delta, end)]
        for inner, (block, r) in enumerate(zip(own, rows)):
            raw = stack_steps(proj_ref, r, 1)
            scale = lax.rsqrt(jnp.sum(raw * raw, axis=1, keepdims=True) + 1e-06)
            keys = raw * scale
            strengths = strengths_of(logit_ref, r, head)
            values = stack_steps(proj_ref, r, 3)
            crossed = tn(
                masked[inner],
                jnp.concatenate([proj_ref[r, 0:DK], (-strengths * keys).astype(BF)], 0),
            )
            d_query = many[inner][:SPAN, ROWS:] + onward[inner][:SPAN]
            inner_sum = many[inner][SPAN:, ROWS:] + onward[inner][SPAN:]
            d_keys = crossed + direct[inner] - strengths * inner_sum
            d_values = strengths * held[inner]
            d_rate = jnp.sum(held[inner] * values - keys * inner_sum, axis=1, keepdims=True)
            d_raw = scale * (d_keys - keys * jnp.sum(keys * d_keys, axis=1, keepdims=True))
            d_logit = d_rate * strengths * (1.0 - 0.5 * strengths)
            out_ref[r, 0:DK] = d_query.astype(BF)
            out_ref[r, DK : 2 * DK] = d_raw[:SPAN].astype(BF)
            out_ref[r, 2 * DK : 3 * DK] = d_raw[SPAN:].astype(BF)
            out_ref[r, 3 * DK : 4 * DK] = d_values[:SPAN].astype(BF)
            out_ref[r, 4 * DK : 5 * DK] = d_values[SPAN:].astype(BF)
            rate_ref[r, :] = jnp.concatenate([d_logit[:SPAN], d_logit[SPAN:]], 1)
        return carry

    lax.fori_loop(0, blocks // unroll, body, 0)


def grad_pass(projected, logits, d_out, kept, edges, head, marks=()):
    tokens = projected.shape[0]
    blocks = tokens // SPAN
    nodes = 2 * blocks - 1
    tile = pl.BlockSpec((1, blocks, ROWS, DK), lambda h: (head, 0, 0, 0))
    branch = pl.BlockSpec((1, nodes, DK, DK), lambda h: (head, 0, 0, 0))
    unroll = divisor(blocks, 4)
    return pl.pallas_call(
        functools.partial(grad_kernel, blocks, unroll, len(marks), head),
        grid=(1,),
        out_shape=(
            jax.ShapeDtypeStruct((tokens, COLS), BF),
            jax.ShapeDtypeStruct((tokens, 2), F32),
        ),
        in_specs=[
            pl.BlockSpec((tokens, COLS), lambda h: (0, head)),
            pl.BlockSpec((tokens, logits.shape[1]), lambda h: (0, 0)),
            pl.BlockSpec((tokens, DK), lambda h: (0, head)),
        ]
        + [tile] * 5
        + [branch] * 3
        + [pl.BlockSpec((1, 2, DK, DK), lambda h: (head, 0, 0, 0))]
        + [pl.BlockSpec(memory_space=pl.ANY)] * len(marks),
        out_specs=(
            pl.BlockSpec((tokens, COLS), lambda h: (0, h)),
            pl.BlockSpec((tokens, 2), lambda h: (0, 0)),
        ),
        scratch_shapes=[
            pltpu.VMEM((nodes, DK, DK), F32),
            pltpu.VMEM((nodes, DK, DK), F32),
        ],
        compiler_params=params(),
        cost_estimate=pl.CostEstimate(
            flops=blocks * 300 * DK**3, bytes_accessed=8 << 20, transcendentals=0
        ),
        name="grad_pass",
    )(projected, logits, d_out, *kept, edges, *marks)


def bmm(a, b):
    return jnp.einsum("hij,hjk->hik", a.astype(BF), b.astype(BF), preferred_element_type=F32)


def bmm_t(a, b):
    return jnp.einsum("hji,hjk->hik", a.astype(BF), b.astype(BF), preferred_element_type=F32)


def shifted(value, by):
    devices = lax.axis_size("seq")
    pairs = [(i, i + by) for i in range(devices) if 0 <= i + by < devices]
    return lax.ppermute(value.astype(BF), "seq", pairs).astype(F32)


def exchange(total):
    devices = lax.axis_size("seq")
    tail_map, tail_shift, head_source = total[:, 0], total[:, 1], total[:, 2]
    head_map = tail_map
    past_map = past_shift = next_map = next_source = None
    by = 1
    while by < devices:
        last = 2 * by >= devices
        if last:
            got_shift = shifted(tail_shift, by)
            got_source = shifted(head_source, -by)
        else:
            behind = shifted(jnp.concatenate([tail_map, tail_shift], 2), by)
            ahead = shifted(jnp.concatenate([head_map, head_source], 2), -by)
            got_map, got_shift = behind[:, :, :DK], behind[:, :, DK:]
            got_next, got_source = ahead[:, :, :DK], ahead[:, :, DK:]
        if past_map is None:
            past_shift, next_source = got_shift, got_source
        else:
            past_shift = past_shift + got_shift + bmm(past_map, got_shift)
            next_source = next_source + got_source + bmm_t(next_map, got_source)
        if not last:
            if past_map is None:
                past_map, next_map = got_map, got_next
            else:
                past_map = past_map + got_map + bmm(past_map, got_map)
                next_map = next_map + got_next + bmm(got_next, next_map)
            tail_shift = tail_shift + got_shift + bmm(tail_map, got_shift)
            head_source = head_source + got_source + bmm_t(head_map, got_source)
            tail_map = tail_map + got_map + bmm(tail_map, got_map)
            head_map = head_map + got_next + bmm(got_next, head_map)
        by *= 2
    return jnp.stack([past_shift, next_source], 1)


def flipped(value, bit):
    devices = lax.axis_size("head")
    return lax.ppermute(value, "head", [(i, i ^ bit) for i in range(devices)])


def line_step(value, stride, count, step, ways):
    pairs = []
    for device in range(lax.axis_size("seq")):
        place = device // stride % count
        for way in ways:
            if 0 <= place + way * step < count:
                pairs.append((device, device + way * stride))
    return lax.ppermute(value.astype(BF), "seq", pairs)


def line_scatter(part, stride, count):
    place = lax.axis_index("seq") // stride % count
    if count == 1:
        return part(place).astype(F32), []
    first = part(jnp.where(2 * place < count, count - 1, 0))
    arrived = line_step(first, stride, count, count - 1, (1, -1))
    if count == 2:
        return part(place).astype(F32) + arrived.astype(F32), [arrived]
    held = {}
    for way in (1, -1):
        held[way] = jnp.where(place == (1 if way == 1 else count - 2), arrived.astype(F32), 0.0)
    for step in range(count - 2, 0, -1):
        came = []
        for way in (1, -1):
            value = part(jnp.clip(place + way * step, 0, count - 1)).astype(F32) + held[way]
            came.append(line_step(value, stride, count, step, (way,)))
            held[way] = came[-1].astype(F32)
        if step == 2:
            before = came
    return part(place).astype(F32) + held[1] + held[-1], before if count > 3 else [arrived]


def side_product(side, grads):
    return lax.dot_general(
        side, grads, (((0,), (0,)), ((), ())), preferred_element_type=F32
    ).astype(BF)


def inner_scatter(sides, grads):
    devices = lax.axis_size("seq")
    inner = sides.shape[0]
    place = lax.axis_index("seq") % inner

    def product(index):
        return side_product(lax.dynamic_index_in_dim(sides, index, 0, keepdims=False), grads)

    if inner == 2:
        leaving = product(1 - place)
        arriving = lax.ppermute(leaving, "seq", [(i, i ^ 1) for i in range(devices)])
        kept = lax.optimization_barrier(product(place))
        return kept, arriving, leaving
    total, unused = line_scatter(product, 1, inner)
    return total, jnp.zeros(total.shape, BF), total


def outer_scatter(total, inner):
    outer = lax.axis_size("seq") // inner
    rows = total.shape[0] // outer
    return line_scatter(
        lambda index: lax.dynamic_slice_in_dim(total, index * rows, rows, 0), inner, outer
    )


def rate_total(part):
    devices = lax.axis_size("seq")
    rows = part.shape[1] // devices
    if devices & (devices - 1):
        return lax.psum_scatter(part.T.astype(BF), "seq", scatter_dimension=0, tiled=True).astype(F32)
    by = 1
    while by < devices:
        got = lax.ppermute(part.astype(BF), "seq", [(i, i ^ by) for i in range(devices)])
        part = part + got.astype(F32)
        by *= 2
    return lax.dynamic_slice_in_dim(part, lax.axis_index("seq") * rows, rows, 1).T


def shards(layer_input, w_proj, w_beta, beta_bias, d_out):
    tokens, features = layer_input.shape
    heads = w_beta.shape[1] // 2
    devices = lax.axis_size("seq")
    spread = lax.axis_size("head")
    if spread == 4:
        index = lax.axis_index("head")
        mate = flipped(layer_input, 1)
        far = flipped(layer_input, 2)
        far_mate = flipped(far, 1)
        whole = jnp.zeros((tokens, spread * features), BF)
        for bit, part in enumerate((layer_input, mate, far, far_mate)):
            whole = lax.dynamic_update_slice_in_dim(whole, part, (index ^ bit) * features, 1)
    else:
        whole = lax.all_gather(layer_input, "head", axis=1, tiled=True)
    logits = jnp.dot(whole, w_beta, preferred_element_type=F32) + beta_bias
    projected = jnp.dot(whole, w_proj, preferred_element_type=F32).astype(BF)
    outer = 4 if devices % 4 == 0 else devices
    inner = devices // outer
    sides = jnp.transpose(
        whole.reshape(tokens, outer, inner, whole.shape[1] // devices), (2, 0, 1, 3)
    ).reshape(inner, tokens, whole.shape[1] // inner)

    *kept, total = local_pass(projected, logits, d_out, heads)
    edges = exchange(total)
    grads, rates, pieces = [], [], []
    early = (heads + 1) // 2
    wait = []
    for head in range(heads):
        grad, rate = grad_pass(
            projected, logits, d_out, kept, edges, head, wait
        )
        grads.append(grad)
        rates.append(rate)
        wait = [rate]
        if head == early - 1:
            sent = side_product(whole, jnp.concatenate(grads, 1))
            weights = [lax.psum_scatter(sent, "seq", scatter_dimension=0, tiled=True).astype(F32)]
            wait = [sent]
        elif early <= head < heads - 1:
            *piece, sent = inner_scatter(sides, grad)
            pieces.append(piece)
            wait = [sent]
    grad_logits = jnp.concatenate(rates, 1).astype(BF)
    grad_beta = rate_total(
        lax.dot_general(
            grad_logits, whole, (((0,), (0,)), ((), ())), preferred_element_type=F32
        )
    )
    grad_projected = jnp.concatenate(grads, 1)

    def input_part(weights, rate_weights):
        return (
            jnp.einsum("tc,dc->td", grad_projected, weights, preferred_element_type=F32)
            + jnp.einsum("tc,dc->td", grad_logits, rate_weights, preferred_element_type=F32)
        ).astype(BF)

    if spread == 4:
        core, chip = index % 2, index // 2
        product = input_part(w_proj, w_beta)

        def columns_of(side):
            return jnp.concatenate(
                [
                    lax.dynamic_slice_in_dim(product, (2 * other + side) * features, features, 1)
                    for other in range(2)
                ],
                1,
            )

        arrived = flipped(columns_of(1 - core), 1)
        own = columns_of(core)
        parts = lax.optimization_barrier(own).astype(F32) + arrived
        leaving = lax.dynamic_slice_in_dim(parts, (1 - chip) * features, features, 1).astype(BF)
        arrived = flipped(leaving, 2)
        grad_input = (
            lax.dynamic_slice_in_dim(parts, chip * features, features, 1) + arrived
        ).astype(BF)
    else:
        grad_input = lax.psum_scatter(
            input_part(w_proj, w_beta), "head", scatter_dimension=1, tiled=True
        )
    for keep, arrived in pieces:
        total, unused = outer_scatter(keep.astype(F32) + arrived.astype(F32), inner)
        weights.append(total)
    if heads > 1:
        total, unused = outer_scatter(side_product(whole, grads[-1]), inner)
        rows = total.shape[0] // inner
        total, unused = line_scatter(
            lambda place: lax.dynamic_slice_in_dim(total, place * rows, rows, 0), 1, inner
        )
        weights.append(total)
    return (grad_input, jnp.concatenate(weights, 1), grad_beta)


def solution(mesh):
    in_specs = (P("seq", "head"), P(None, "head"), P(None, "head"), P("head"), P("seq", "head"))
    out_specs = (P("seq", "head"), P("seq", "head"), P("seq", "head"))
    return jax.shard_map(shards, mesh=mesh, in_specs=in_specs, out_specs=out_specs, check_vma=False)
```

```python
import functools

import jax
import jax.numpy as jnp
import numpy as np
from jax import lax
from jax.experimental import pallas as pl
from jax.experimental.pallas import tpu as pltpu
from jax.sharding import PartitionSpec as P

DK = 128
SPAN = 64
ROWS = 2 * SPAN
BASE = 16
HALF = BASE // 2
COLS = 5 * DK
BF = jnp.bfloat16
F32 = jnp.float32
VMEM_LIMIT = 56 << 20


def dot(a, b, ca, cb):
    return lax.dot_general(
        a.astype(BF), b.astype(BF), (((ca,), (cb,)), ((), ())), preferred_element_type=F32
    )


def nn(a, b):
    return dot(a, b, 1, 0)


def nt(a, b):
    return dot(a, b, 1, 1)


def tn(a, b):
    return dot(a, b, 0, 0)


def split(a):
    high = a.astype(BF)
    return high, (a - high.astype(F32)).astype(BF)


def nn3(a, b):
    ah, al = split(a)
    bh, bl = split(b)
    return nn(jnp.concatenate([ah, al], 1), jnp.concatenate([bh, bh], 0)) + nn(ah, bl)


def nt3(a, b):
    ah, al = split(a)
    bh, bl = split(b)
    return nt(jnp.concatenate([ah, al], 1), jnp.concatenate([bh, bh], 1)) + nt(ah, bl)


def rows_cols(rows, cols):
    row = lax.broadcasted_iota(jnp.int32, (rows, cols), 0)
    col = lax.broadcasted_iota(jnp.int32, (rows, cols), 1)
    return row, col


def order(index):
    return 2 * (index % SPAN) + index // SPAN


def strict_mask():
    row, col = rows_cols(ROWS, ROWS)
    return order(col) < order(row)


def visible_mask():
    row, col = rows_cols(SPAN, ROWS)
    return col % SPAN <= row


def stack_steps(ref, rows, first):
    return jnp.concatenate(
        [ref[rows, first * DK : (first + 1) * DK], ref[rows, (first + 1) * DK : (first + 2) * DK]], 0
    ).astype(F32)


def strengths_of(logit_ref, rows, head):
    pair = logit_ref[rows, 2 * head : 2 * head + 2]
    return 2.0 * jax.nn.sigmoid(jnp.concatenate([pair[:, 0:1], pair[:, 1:2]], 0))


def spread_table():
    table = np.zeros((DK, BASE, DK), np.float32)
    for lane in range(DK):
        group = (lane % SPAN) // HALF
        for member in range(BASE):
            source = (member // HALF) * SPAN + group * HALF + member % HALF
            table[source, member, lane] = 1.0
    return table.reshape(DK, BASE * DK)


def local_kernel(
    blocks,
    unroll,
    heads,
    spread_ref,
    proj_ref,
    logit_ref,
    grad_ref,
    key_ref,
    inv_ref,
    wide_ref,
    upd_ref,
    read_ref,
    map_ref,
    shift_ref,
    source_ref,
    total_ref,
    system,
    packed,
    coef,
    solved,
    maps,
    shifts,
    sources,
    rates,
):
    for head in range(heads):

        @pl.when(pl.program_id(0) == head)
        def take(head=head):
            rates[...] = logit_ref[:, 2 * head : 2 * head + 2]

    strict = strict_mask()
    lane_group = (rows_cols(HALF, ROWS)[1] % SPAN) // HALF

    def first(outer, carry):
        for inner in range(unroll):
            block = outer * unroll + inner
            rows = pl.ds(pl.multiple_of(block * SPAN, SPAN), SPAN)
            raw = stack_steps(proj_ref, rows, 1)
            strengths = strengths_of(rates, rows, 0)
            keys = raw * lax.rsqrt(jnp.sum(raw * raw, axis=1, keepdims=True) + 1e-06)
            key_ref[0, block] = keys.astype(BF)
            lower = jnp.where(strict, strengths * nt3(keys, keys), 0.0)
            system[block] = lower
            for step in range(2):
                piece = jnp.zeros((HALF, ROWS), F32)
                for group in range(SPAN // HALF):
                    start = step * SPAN + group * HALF
                    piece = jnp.where(lane_group == group, lower[start : start + HALF], piece)
                packed[pl.ds(step * HALF * blocks + block, HALF, stride=blocks), :] = piece
        return carry

    lax.fori_loop(0, blocks // unroll, first, 0)

    high, low = split(packed[...])
    spread = spread_ref[...]
    coef[...] = nn(jnp.concatenate([high, low], 1), jnp.concatenate([spread, spread], 0))
    lane = rows_cols(blocks, ROWS)[1]
    found = {}
    for when in range(BASE):
        step, tick = when % 2, when // 2
        here = step * HALF + tick
        value = jnp.where((lane // SPAN == step) & (lane % HALF == tick), 1.0, 0.0)
        for before in range(when):
            there = (before % 2) * HALF + before // 2
            weight = coef[here * blocks : (here + 1) * blocks, there * ROWS : (there + 1) * ROWS]
            value = value - weight * found[before]
        found[when] = value
        solved[here * blocks : (here + 1) * blocks, :] = value

    row, col = rows_cols(ROWS, ROWS)
    row_time, col_time = order(row), order(col)
    visible = visible_mask()

    joins = []
    size = BASE
    while size < ROWS:
        joins.append(
            (row_time // (2 * size) == col_time // (2 * size))
            & (row_time // size != col_time // size)
        )
        size *= 2

    def second(outer, carry):
        own = [outer * unroll + inner for inner in range(unroll)]
        rows = [pl.ds(pl.multiple_of(block * SPAN, SPAN), SPAN) for block in own]
        inverse = []
        for block in own:
            pieces = []
            for step in range(2):
                piece = solved[pl.ds(step * HALF * blocks + block, HALF, stride=blocks), :]
                for group in range(SPAN // HALF):
                    pieces.append(jnp.where(lane_group == group, piece, 0.0))
            inverse.append(jnp.concatenate(pieces, 0))
        for join in joins:
            half = [
                nn3(jnp.where(join, system[block], 0.0), inv) for block, inv in zip(own, inverse)
            ]
            inverse = [inv - nn3(inv, x) for inv, x in zip(inverse, half)]
        inverse = [inv.astype(BF) for inv in inverse]
        scores = [
            jnp.where(visible, nt(proj_ref[r, 0:DK], key_ref[0, block]), 0.0).astype(BF)
            for block, r in zip(own, rows)
        ]
        reads = [tn(score, grad_ref[r, :]).astype(BF) for score, r in zip(scores, rows)]
        both = []
        for block, r, inv in zip(own, rows, inverse):
            inv_ref[0, block] = inv
            strengths = strengths_of(rates, r, 0)
            keys = key_ref[0, block].astype(F32)
            values = stack_steps(proj_ref, r, 3)
            targets = jnp.concatenate([strengths * keys, strengths * values], 1)
            both.append(nn(inv, targets).astype(BF))
        folded = [tn(key_ref[0, block], x) for block, x in zip(own, both)]
        gained = [
            tn(proj_ref[r, 0:DK], grad_ref[r, :]) - tn(x[:, :DK], read)
            for r, x, read in zip(rows, both, reads)
        ]
        for block, x, read, fold, gain in zip(own, both, reads, folded, gained):
            wide_ref[0, block] = x[:, :DK]
            upd_ref[0, block] = x[:, DK:]
            read_ref[0, block] = read
            maps[block] = -fold[:, :DK]
            shifts[block] = fold[:, DK:]
            sources[block] = gain
        return carry

    lax.fori_loop(0, blocks // unroll, second, 0)

    offset, count = 0, blocks
    while count > 1:
        half = count // 2
        lefts = [offset + 2 * pair for pair in range(half)]
        joined = [
            nn(maps[left + 1], jnp.concatenate([maps[left], shifts[left]], 1)) for left in lefts
        ]
        moved = [tn(maps[left], sources[left + 1]) for left in lefts]
        for pair, left in enumerate(lefts):
            parent = offset + count + pair
            maps[parent] = maps[left] + maps[left + 1] + joined[pair][:, :DK]
            shifts[parent] = shifts[left] + shifts[left + 1] + joined[pair][:, DK:]
            sources[parent] = sources[left] + sources[left + 1] + moved[pair]
        offset += count
        count //= 2
    map_ref[0] = maps[...].astype(BF)
    shift_ref[0] = shifts[...].astype(BF)
    source_ref[0] = sources[...].astype(BF)
    total_ref[0, 0] = maps[offset]
    total_ref[0, 1] = shifts[offset]
    total_ref[0, 2] = sources[offset]


def divisor(blocks, most):
    while blocks % most:
        most //= 2
    return most


def params():
    return pltpu.CompilerParams(
        dimension_semantics=("arbitrary",), vmem_limit_bytes=VMEM_LIMIT
    )


def local_pass(projected, logits, d_out, heads):
    tokens = projected.shape[0]
    blocks = tokens // SPAN
    nodes = 2 * blocks - 1
    square = jax.ShapeDtypeStruct((heads, blocks, ROWS, DK), BF)
    tree = jax.ShapeDtypeStruct((heads, nodes, DK, DK), BF)
    tile = pl.BlockSpec((1, blocks, ROWS, DK), lambda h: (h, 0, 0, 0))
    branch = pl.BlockSpec((1, nodes, DK, DK), lambda h: (h, 0, 0, 0))
    unroll = divisor(blocks, 16)
    return pl.pallas_call(
        functools.partial(local_kernel, blocks, unroll, heads),
        grid=(heads,),
        out_shape=(square,) * 5
        + (tree,) * 3
        + (jax.ShapeDtypeStruct((heads, 3, DK, DK), F32),),
        in_specs=[
            pl.BlockSpec((DK, BASE * DK), lambda h: (0, 0)),
            pl.BlockSpec((tokens, COLS), lambda h: (0, h)),
            pl.BlockSpec((tokens, logits.shape[1]), lambda h: (0, 0)),
            pl.BlockSpec((tokens, DK), lambda h: (0, h)),
        ],
        out_specs=(tile,) * 5
        + (branch,) * 3
        + (pl.BlockSpec((1, 3, DK, DK), lambda h: (h, 0, 0, 0)),),
        scratch_shapes=[
            pltpu.VMEM((blocks, ROWS, ROWS), F32),
            pltpu.VMEM((BASE * blocks, ROWS), F32),
            pltpu.VMEM((BASE * blocks, BASE * ROWS), F32),
            pltpu.VMEM((BASE * blocks, ROWS), F32),
            pltpu.VMEM((nodes, DK, DK), F32),
            pltpu.VMEM((nodes, DK, DK), F32),
            pltpu.VMEM((nodes, DK, DK), F32),
            pltpu.VMEM((tokens, 2), F32),
        ],
        compiler_params=params(),
        cost_estimate=pl.CostEstimate(
            flops=heads * blocks * 270 * DK**3, bytes_accessed=heads * 8 << 20, transcendentals=0
        ),
        name="local_pass",
    )(jnp.asarray(spread_table(), BF), projected, logits, d_out)


def grad_kernel(
    blocks,
    unroll,
    marks,
    head,
    proj_ref,
    logit_ref,
    grad_ref,
    key_ref,
    inv_ref,
    wide_ref,
    upd_ref,
    read_ref,
    map_ref,
    shift_ref,
    source_ref,
    edge_ref,
    *rest,
):
    out_ref, rate_ref, states, ends = rest[marks:]
    nodes = 2 * blocks - 1
    states[nodes - 1] = edge_ref[0, 0]
    ends[nodes - 1] = edge_ref[0, 1]
    count, offset = 2, nodes - 3
    while count <= blocks:
        pairs = [(offset + 2 * pair, offset + count + pair) for pair in range(count // 2)]
        onward = [nn(map_ref[0, left], states[parent]) for left, parent in pairs]
        backward = [tn(map_ref[0, left + 1], ends[parent]) for left, parent in pairs]
        for (left, parent), ahead, behind in zip(pairs, onward, backward):
            state, end = states[parent], ends[parent]
            states[left] = state
            states[left + 1] = state + ahead + shift_ref[0, left].astype(F32)
            ends[left + 1] = end
            ends[left] = end + behind + source_ref[0, left + 1].astype(F32)
        count *= 2
        offset -= count

    strict = strict_mask()
    visible = visible_mask()

    def body(outer, carry):
        own = [outer * unroll + inner for inner in range(unroll)]
        rows = [pl.ds(pl.multiple_of(block * SPAN, SPAN), SPAN) for block in own]
        state = [states[block].astype(BF) for block in own]
        end = [ends[block].astype(BF) for block in own]
        back = [
            (read_ref[0, block].astype(F32) + nn(key_ref[0, block], e)).astype(BF)
            for block, e in zip(own, end)
        ]
        delta = [
            (upd_ref[0, block].astype(F32) - nn(wide_ref[0, block], s)).astype(BF)
            for block, s in zip(own, state)
        ]
        held = [tn(inv_ref[0, block], b) for block, b in zip(own, back)]
        many = [
            nt(
                jnp.concatenate([grad_ref[r, :], h.astype(BF)], 0),
                jnp.concatenate([d, s], 0),
            )
            for r, h, d, s in zip(rows, held, delta, state)
        ]
        masked = [
            jnp.concatenate(
                [
                    jnp.where(visible, m[:SPAN, :ROWS], 0.0),
                    jnp.where(strict, m[SPAN:, :ROWS], 0.0),
                ],
                0,
            ).astype(BF)
            for m in many
        ]
        onward = [nn(m, key_ref[0, block]) for block, m in zip(own, masked)]
        direct = [nt(d, e) for d, e in zip(delta, end)]
        for inner, (block, r) in enumerate(zip(own, rows)):
            raw = stack_steps(proj_ref, r, 1)
            scale = lax.rsqrt(jnp.sum(raw * raw, axis=1, keepdims=True) + 1e-06)
            keys = raw * scale
            strengths = strengths_of(logit_ref, r, head)
            values = stack_steps(proj_ref, r, 3)
            crossed = tn(
                masked[inner],
                jnp.concatenate([proj_ref[r, 0:DK], (-strengths * keys).astype(BF)], 0),
            )
            d_query = many[inner][:SPAN, ROWS:] + onward[inner][:SPAN]
            inner_sum = many[inner][SPAN:, ROWS:] + onward[inner][SPAN:]
            d_keys = crossed + direct[inner] - strengths * inner_sum
            d_values = strengths * held[inner]
            d_rate = jnp.sum(held[inner] * values - keys * inner_sum, axis=1, keepdims=True)
            d_raw = scale * (d_keys - keys * jnp.sum(keys * d_keys, axis=1, keepdims=True))
            d_logit = d_rate * strengths * (1.0 - 0.5 * strengths)
            out_ref[r, 0:DK] = d_query.astype(BF)
            out_ref[r, DK : 2 * DK] = d_raw[:SPAN].astype(BF)
            out_ref[r, 2 * DK : 3 * DK] = d_raw[SPAN:].astype(BF)
            out_ref[r, 3 * DK : 4 * DK] = d_values[:SPAN].astype(BF)
            out_ref[r, 4 * DK : 5 * DK] = d_values[SPAN:].astype(BF)
            rate_ref[r, :] = jnp.concatenate([d_logit[:SPAN], d_logit[SPAN:]], 1)
        return carry

    lax.fori_loop(0, blocks // unroll, body, 0)


def grad_pass(projected, logits, d_out, kept, edges, head, marks=()):
    tokens = projected.shape[0]
    blocks = tokens // SPAN
    nodes = 2 * blocks - 1
    tile = pl.BlockSpec((1, blocks, ROWS, DK), lambda h: (head, 0, 0, 0))
    branch = pl.BlockSpec((1, nodes, DK, DK), lambda h: (head, 0, 0, 0))
    unroll = divisor(blocks, 4)
    return pl.pallas_call(
        functools.partial(grad_kernel, blocks, unroll, len(marks), head),
        grid=(1,),
        out_shape=(
            jax.ShapeDtypeStruct((tokens, COLS), BF),
            jax.ShapeDtypeStruct((tokens, 2), F32),
        ),
        in_specs=[
            pl.BlockSpec((tokens, COLS), lambda h: (0, head)),
            pl.BlockSpec((tokens, logits.shape[1]), lambda h: (0, 0)),
            pl.BlockSpec((tokens, DK), lambda h: (0, head)),
        ]
        + [tile] * 5
        + [branch] * 3
        + [pl.BlockSpec((1, 2, DK, DK), lambda h: (head, 0, 0, 0))]
        + [pl.BlockSpec(memory_space=pl.ANY)] * len(marks),
        out_specs=(
            pl.BlockSpec((tokens, COLS), lambda h: (0, h)),
            pl.BlockSpec((tokens, 2), lambda h: (0, 0)),
        ),
        scratch_shapes=[
            pltpu.VMEM((nodes, DK, DK), F32),
            pltpu.VMEM((nodes, DK, DK), F32),
        ],
        compiler_params=params(),
        cost_estimate=pl.CostEstimate(
            flops=blocks * 300 * DK**3, bytes_accessed=8 << 20, transcendentals=0
        ),
        name="grad_pass",
    )(projected, logits, d_out, *kept, edges, *marks)


def bmm(a, b):
    return jnp.einsum("hij,hjk->hik", a.astype(BF), b.astype(BF), preferred_element_type=F32)


def bmm_t(a, b):
    return jnp.einsum("hji,hjk->hik", a.astype(BF), b.astype(BF), preferred_element_type=F32)


def shifted(value, by):
    devices = lax.axis_size("seq")
    pairs = [(i, i + by) for i in range(devices) if 0 <= i + by < devices]
    return lax.ppermute(value.astype(BF), "seq", pairs).astype(F32)


def exchange(total):
    devices = lax.axis_size("seq")
    tail_map, tail_shift, head_source = total[:, 0], total[:, 1], total[:, 2]
    head_map = tail_map
    past_map = past_shift = next_map = next_source = None
    by = 1
    while by < devices:
        last = 2 * by >= devices
        if last:
            got_shift = shifted(tail_shift, by)
            got_source = shifted(head_source, -by)
        else:
            behind = shifted(jnp.concatenate([tail_map, tail_shift], 2), by)
            ahead = shifted(jnp.concatenate([head_map, head_source], 2), -by)
            got_map, got_shift = behind[:, :, :DK], behind[:, :, DK:]
            got_next, got_source = ahead[:, :, :DK], ahead[:, :, DK:]
        if past_map is None:
            past_shift, next_source = got_shift, got_source
        else:
            past_shift = past_shift + got_shift + bmm(past_map, got_shift)
            next_source = next_source + got_source + bmm_t(next_map, got_source)
        if not last:
            if past_map is None:
                past_map, next_map = got_map, got_next
            else:
                past_map = past_map + got_map + bmm(past_map, got_map)
                next_map = next_map + got_next + bmm(got_next, next_map)
            tail_shift = tail_shift + got_shift + bmm(tail_map, got_shift)
            head_source = head_source + got_source + bmm_t(head_map, got_source)
            tail_map = tail_map + got_map + bmm(tail_map, got_map)
            head_map = head_map + got_next + bmm(got_next, head_map)
        by *= 2
    return jnp.stack([past_shift, next_source], 1)


def flipped(value, bit):
    devices = lax.axis_size("head")
    return lax.ppermute(value, "head", [(i, i ^ bit) for i in range(devices)])


def line_step(value, stride, count, step, ways):
    pairs = []
    for device in range(lax.axis_size("seq")):
        place = device // stride % count
        for way in ways:
            if 0 <= place + way * step < count:
                pairs.append((device, device + way * stride))
    return lax.ppermute(value.astype(BF), "seq", pairs)


def line_scatter(part, stride, count):
    place = lax.axis_index("seq") // stride % count
    if count == 1:
        return part(place).astype(F32), []
    first = part(jnp.where(2 * place < count, count - 1, 0))
    arrived = line_step(first, stride, count, count - 1, (1, -1))
    if count == 2:
        return part(place).astype(F32) + arrived.astype(F32), [arrived]
    held = {}
    for way in (1, -1):
        held[way] = jnp.where(place == (1 if way == 1 else count - 2), arrived.astype(F32), 0.0)
    for step in range(count - 2, 0, -1):
        came = []
        for way in (1, -1):
            value = part(jnp.clip(place + way * step, 0, count - 1)).astype(F32) + held[way]
            came.append(line_step(value, stride, count, step, (way,)))
            held[way] = came[-1].astype(F32)
        if step == 2:
            before = came
    return part(place).astype(F32) + held[1] + held[-1], before if count > 3 else [arrived]


def side_product(side, grads):
    return lax.dot_general(
        side, grads, (((0,), (0,)), ((), ())), preferred_element_type=F32
    ).astype(BF)


def inner_scatter(sides, grads):
    devices = lax.axis_size("seq")
    inner = sides.shape[0]
    place = lax.axis_index("seq") % inner

    def product(index):
        return side_product(lax.dynamic_index_in_dim(sides, index, 0, keepdims=False), grads)

    if inner == 2:
        leaving = product(1 - place)
        arriving = lax.ppermute(leaving, "seq", [(i, i ^ 1) for i in range(devices)])
        kept = lax.optimization_barrier(product(place))
        return kept, arriving, leaving
    total, unused = line_scatter(product, 1, inner)
    return total, jnp.zeros(total.shape, BF), total


def outer_scatter(total, inner):
    outer = lax.axis_size("seq") // inner
    rows = total.shape[0] // outer
    return line_scatter(
        lambda index: lax.dynamic_slice_in_dim(total, index * rows, rows, 0), inner, outer
    )


def rate_total(part):
    devices = lax.axis_size("seq")
    rows = part.shape[1] // devices
    if devices & (devices - 1):
        return lax.psum_scatter(part.T.astype(BF), "seq", scatter_dimension=0, tiled=True).astype(F32)
    by = 1
    while by < devices:
        got = lax.ppermute(part.astype(BF), "seq", [(i, i ^ by) for i in range(devices)])
        part = part + got.astype(F32)
        by *= 2
    return lax.dynamic_slice_in_dim(part, lax.axis_index("seq") * rows, rows, 1).T


def shards(layer_input, w_proj, w_beta, beta_bias, d_out):
    tokens, features = layer_input.shape
    heads = w_beta.shape[1] // 2
    devices = lax.axis_size("seq")
    spread = lax.axis_size("head")
    if spread == 4:
        index = lax.axis_index("head")
        mate = flipped(layer_input, 1)
        far = flipped(layer_input, 2)
        far_mate = flipped(far, 1)
        whole = jnp.zeros((tokens, spread * features), BF)
        for bit, part in enumerate((layer_input, mate, far, far_mate)):
            whole = lax.dynamic_update_slice_in_dim(whole, part, (index ^ bit) * features, 1)
    else:
        whole = lax.all_gather(layer_input, "head", axis=1, tiled=True)
    logits = jnp.dot(whole, w_beta, preferred_element_type=F32) + beta_bias
    projected = jnp.dot(whole, w_proj, preferred_element_type=F32).astype(BF)
    outer = 4 if devices % 4 == 0 else devices
    inner = devices // outer
    sides = jnp.transpose(
        whole.reshape(tokens, outer, inner, whole.shape[1] // devices), (2, 0, 1, 3)
    ).reshape(inner, tokens, whole.shape[1] // inner)

    *kept, total = local_pass(projected, logits, d_out, heads)
    edges = exchange(total)
    grads, rates, pieces = [], [], []
    early = (heads + 1) // 2
    wait = []
    for head in range(heads):
        grad, rate = grad_pass(
            projected, logits, d_out, kept, edges, head, wait
        )
        grads.append(grad)
        rates.append(rate)
        wait = [rate]
        if head == early - 1:
            sent = side_product(whole, jnp.concatenate(grads, 1))
            weights = [lax.psum_scatter(sent, "seq", scatter_dimension=0, tiled=True).astype(F32)]
            wait = [sent]
        elif early <= head < heads - 1:
            *piece, sent = inner_scatter(sides, grad)
            pieces.append(piece)
            wait = []
    grad_logits = jnp.concatenate(rates, 1).astype(BF)
    grad_beta = rate_total(
        lax.dot_general(
            grad_logits, whole, (((0,), (0,)), ((), ())), preferred_element_type=F32
        )
    )
    grad_projected = jnp.concatenate(grads, 1)

    def input_part(weights, rate_weights):
        return (
            jnp.einsum("tc,dc->td", grad_projected, weights, preferred_element_type=F32)
            + jnp.einsum("tc,dc->td", grad_logits, rate_weights, preferred_element_type=F32)
        ).astype(BF)

    if spread == 4:
        core, chip = index % 2, index // 2
        product = input_part(w_proj, w_beta)

        def columns_of(side):
            return jnp.concatenate(
                [
                    lax.dynamic_slice_in_dim(product, (2 * other + side) * features, features, 1)
                    for other in range(2)
                ],
                1,
            )

        arrived = flipped(columns_of(1 - core), 1)
        own = columns_of(core)
        parts = lax.optimization_barrier(own).astype(F32) + arrived
        leaving = lax.dynamic_slice_in_dim(parts, (1 - chip) * features, features, 1).astype(BF)
        arrived = flipped(leaving, 2)
        grad_input = (
            lax.dynamic_slice_in_dim(parts, chip * features, features, 1) + arrived
        ).astype(BF)
    else:
        grad_input = lax.psum_scatter(
            input_part(w_proj, w_beta), "head", scatter_dimension=1, tiled=True
        )
    for keep, arrived in pieces:
        total, unused = outer_scatter(keep.astype(F32) + arrived.astype(F32), inner)
        weights.append(total)
    if heads > 1:
        total, unused = outer_scatter(side_product(whole, grads[-1]), inner)
        rows = total.shape[0] // inner
        total, unused = line_scatter(
            lambda place: lax.dynamic_slice_in_dim(total, place * rows, rows, 0), 1, inner
        )
        weights.append(total)
    return (grad_input, jnp.concatenate(weights, 1), grad_beta)


def solution(mesh):
    in_specs = (P("seq", "head"), P(None, "head"), P(None, "head"), P("head"), P("seq", "head"))
    out_specs = (P("seq", "head"), P("seq", "head"), P("seq", "head"))
    return jax.shard_map(shards, mesh=mesh, in_specs=in_specs, out_specs=out_specs, check_vma=False)
```
